32 devices in a mesh: case: 2 (over y), filt: 16 (over z, x, core).
Axes of the slice: x: 2, y: 2, z: 4, core: 2. Of those that a mesh axis runs over, the one named last changes fastest.
Arguments:
- inputs: bfloat16 [2048, 2304], P('filt', 'case'), may hold values from -6 to 6
- weight: bfloat16 [9, 2048, 2048], P(None, 'filt'), may hold values from -0.046875 to 0.046875
- bias_vector: float32 [2048], P('filt'), may hold values from -3 to 3
- cotangent: bfloat16 [2048, 2304], P('filt', 'case'), may hold values from -64 to 64
Outputs:
- activated: bfloat16 [2048, 2304], P('filt', 'case')
- input_grad: bfloat16 [2048, 2304], P('filt', 'case')
- weight_grad: float32 [9, 2048, 2048], P(None, 'filt')
- bias_grad: float32 [2048], P('filt')
The draws below stay inside these ranges and needn't reach their ends.
All inputs are finite; a program needn't handle non-finite values.
Results may differ from the reference program's by a relative error of at most 0.0075.
Values may be sent and summed in bfloat16 or wider, within the bound.
No kernel may reach another device: no remote copies, remote signals or barrier semaphores. Data moves between devices by JAX's collectives and lax.ppermute only.
A program may use at most 192 MiB of HBM per device.

```python
import jax
import jax.numpy as jnp
from jax import lax

C = 2048
GRID = 24
CASES = 4
POS = 2304


def draw_cotangent(key, part):
    first, second = jax.random.split(key, 2)
    position = jnp.arange(POS, dtype=jnp.float32)
    ramp = jnp.exp(jnp.log(3.0) * position / max(POS - 1, 1))
    channel = jnp.exp(jax.random.uniform(second, (C, 1), jnp.float32) * jnp.log(10.0))
    base = jax.random.normal(first, (C, POS), jnp.float32)
    return (0.25 * base * ramp[None, :] * channel).astype(jnp.bfloat16)


def steps_of(own_key, shape, pieces, smallest, largest):
    level = 1.0
    for axis_at, shards_of in pieces:
        draws = jax.random.uniform(jax.random.fold_in(jax.random.fold_in(own_key, 6), axis_at), (shards_of,), jnp.float32, smallest / len(pieces), largest / len(pieces))
        level = level * jnp.repeat(jnp.exp(draws), shape[axis_at] // shards_of).reshape((-1,) + (1,) * (len(shape) - 1 - axis_at))
    return level


def bell_draw(stream_key, dims, deviation, reach, pieces=(), kind=jnp.bfloat16):
    entries = deviation * jax.random.normal(stream_key, dims, jnp.float32)
    if pieces:
        entries = entries * steps_of(stream_key, dims, pieces, -0.22, 0.18)
    return jnp.clip(entries, -reach, reach).astype(kind)


def setup_inputs(seed: int = 0) -> dict:
    keys = jax.random.split(jax.random.key(seed), 5)
    inputs = bell_draw(keys[0], (C, POS), 1.0, 6.0, ((0, 16), (1, 2)))
    weight = bell_draw(keys[1], (9, C, C), (9 * C) ** -0.5, 0.046875, ((1, 16),))
    bias_vector = bell_draw(keys[2], (C,), 0.5, 3.0, ((0, 16),), jnp.float32)
    cotangent = draw_cotangent(jax.random.fold_in(keys[4], 71), 0)
    return dict(inputs=inputs, weight=weight, bias_vector=bias_vector, cotangent=cotangent)


tap_offsets = ((-1, -1), (-1, 0), (-1, 1), (0, -1), (0, 0), (0, 1), (1, -1), (1, 0), (1, 1))


def displace(source, row_step, col_step):
    length = source.shape[1]
    position = jnp.arange(length, dtype=jnp.int32)
    col_index = position % GRID
    row_index = (position // GRID) % GRID
    margin = GRID + 1
    padded = jnp.pad(source, ((0, 0), (margin, margin)))
    begin = margin + row_step * GRID + col_step
    shifted = padded[:, begin:begin + length]
    inside = (row_index + row_step >= 0) & (row_index + row_step < GRID) & (col_index + col_step >= 0) & (col_index + col_step < GRID)
    return jnp.where(inside[None, :], shifted, jnp.zeros((), source.dtype))


def reference(inputs, weight, bias_vector, cotangent):
    preact = jnp.zeros((weight.shape[1], inputs.shape[1]), jnp.float32)
    for tap_index, (row_step, col_step) in enumerate(tap_offsets):
        preact = preact + jnp.dot(weight[tap_index], displace(inputs, row_step, col_step), preferred_element_type=jnp.float32)
    preact = preact + bias_vector.astype(jnp.float32)[:, None]
    gating = jax.nn.sigmoid(preact)
    activated = (preact * gating).astype(jnp.bfloat16)
    grad_pre = (cotangent.astype(jnp.float32) * gating * (1.0 + preact * (1.0 - gating))).astype(jnp.bfloat16)
    backward = jnp.zeros(inputs.shape, jnp.float32)
    weight_list = []
    for tap_index, (row_step, col_step) in enumerate(tap_offsets):
        product = lax.dot_general(weight[tap_index], grad_pre, (((0,), (0,)), ((), ())), preferred_element_type=jnp.float32)
        backward = backward + displace(product, -row_step, -col_step)
        weight_list.append(lax.dot_general(grad_pre, displace(inputs, row_step, col_step), (((1,), (1,)), ((), ())), preferred_element_type=jnp.float32))
    input_grad = backward.astype(jnp.bfloat16)
    weight_grad = jnp.stack(weight_list) / CASES
    bias_grad = jnp.sum(grad_pre.astype(jnp.float32), axis=1) / CASES
    return activated, input_grad, weight_grad, bias_grad
```

```python
import functools

import jax
import jax.numpy as jnp
import numpy as np
from jax import lax
from jax.experimental import pallas as pl
from jax.experimental.pallas import tpu as pltpu
from jax.sharding import PartitionSpec as P

GRID = 24
TAPS = tuple((a, b) for a in (-1, 0, 1) for b in (-1, 0, 1))
PAD = 32
F32 = jnp.float32
BF16 = jnp.bfloat16
VMEM_LIMIT = 56 * 1024 * 1024


def chip_cycle(chips):
    rows = 4
    cols = chips // rows
    walk = [(r, 0) for r in range(rows)]
    for r in reversed(range(rows)):
        across = range(1, cols) if (rows - 1 - r) % 2 == 0 else reversed(range(1, cols))
        walk += [(r, c) for c in across]
    return [r * cols + c for r, c in walk]


def inside(i, j, a, b):
    keep = None
    for index, step in ((i, a), (j, b)):
        if step:
            ok = index >= 1 if step < 0 else index < GRID - 1
            keep = ok if keep is None else keep & ok
    return keep


def wide(keep, lanes):
    return jnp.concatenate([keep] * (lanes // keep.shape[1]), axis=1) if lanes > keep.shape[1] else keep[:, :lanes]


def forward_kernel(blocks, last, q_ref, *refs):
    refs = list(refs)
    xs = [refs.pop(0) for _ in range(blocks)]
    wo = [refs.pop(0) for _ in range(blocks)]
    ws = [refs.pop(0) for _ in range(blocks)]
    ij = refs.pop(0)
    carry = refs.pop(0) if last else None
    if last:
        bias, cot_own, cot_sib = refs.pop(0), refs.pop(0), refs.pop(0)
        act_own, act_sib, g_own, g_sib, g9_own, g9_sib = (refs.pop(0) for _ in range(6))
        acc, field = refs
    else:
        acc, field = refs
    k = pl.program_id(0)
    cells = acc.shape[0]
    lanes = acc.shape[1]
    part = lanes // 2

    @pl.when(k == 0)
    def _():
        acc_start = carry[...] if last else jnp.zeros(acc.shape, F32)
        acc[...] = acc_start
        field[0:PAD, :] = jnp.zeros((PAD, lanes), F32)
        field[PAD + cells : PAD + cells + PAD, :] = jnp.zeros((PAD, lanes), F32)

    total = None
    for x, w0, w1 in zip(xs, wo, ws):
        w = jnp.concatenate([w0[0], w1[0]], axis=0)
        y = lax.dot_general(x[...], w, (((1,), (1,)), ((), ())), preferred_element_type=F32)
        total = y if total is None else total + y
    field[PAD : PAD + cells, :] = total
    i, j = ij[0], ij[1]
    for t, (a, b) in enumerate(TAPS):

        @pl.when(k == t)
        def _(a=a, b=b):
            start = PAD + a * GRID + b
            moved = field[start : start + cells, :]
            keep = inside(i, j, a, b)
            if keep is not None:
                moved = jnp.where(wide(keep, lanes), moved, 0.0)
            acc[...] += moved

    if last:

        @pl.when(k == len(TAPS) - 1)
        def _():
            for n, (cot, act, g, g9) in enumerate(
                ((cot_own, act_own, g_own, g9_own), (cot_sib, act_sib, g_sib, g9_sib))
            ):
                cols = slice(n * part, (n + 1) * part)
                preact = acc[:, cols] + bias[0:1, cols]
                gate = jax.nn.sigmoid(preact)
                act[...] = (preact * gate).astype(BF16)
                grad = (cot[...].astype(F32) * gate * (1.0 + preact * (1.0 - gate))).astype(BF16)
                g[...] = grad
                field[PAD : PAD + cells, cols] = grad.astype(F32)
            for t, (a, b) in enumerate(TAPS):
                start = PAD - a * GRID - b
                moved = field[start : start + cells, :]
                keep = inside(i, j, -a, -b)
                if keep is not None:
                    moved = jnp.where(wide(keep, lanes), moved, 0.0)
                moved = moved.astype(BF16)
                g9_own[:, t * part : (t + 1) * part] = moved[:, :part]
                g9_sib[:, t * part : (t + 1) * part] = moved[:, part:]


def forward_call(q, ids, xs, w_own, w_sib, ij, extra=None):
    blocks = len(ids)
    cells, lanes = xs[0].shape
    part = w_own.shape[1]
    last = extra is not None
    whole = lambda shape: pl.BlockSpec(shape, lambda k, q: (0,) * len(shape))
    w_specs = [
        pl.BlockSpec((1, part, lanes), functools.partial(lambda n, k, q: (k, 0, q[n]), n)) for n in ids
    ]
    in_specs = [whole((cells, lanes))] * blocks + w_specs + w_specs + [whole(ij.shape)]
    args = list(xs) + [w_own] * blocks + [w_sib] * blocks + [ij]
    if last:
        carry, bias, cot_own, cot_sib = extra
        args += [carry, bias, cot_own, cot_sib]
        in_specs += [whole(v.shape) for v in (carry, bias, cot_own, cot_sib)]
        piece = jax.ShapeDtypeStruct((cells, part), BF16)
        nine = jax.ShapeDtypeStruct((cells, len(TAPS) * part), BF16)
        out_shape = [piece, piece, piece, piece, nine, nine]
        out_specs = [whole(s.shape) for s in out_shape]
        scratch = [pltpu.VMEM((cells, 2 * part), F32)]
    else:
        out_shape = jax.ShapeDtypeStruct((cells, 2 * part), F32)
        out_specs = whole(out_shape.shape)
        scratch = []
    scratch = scratch + [pltpu.VMEM((cells + 2 * PAD, 2 * part), F32)]
    flops = 2 * blocks * cells * lanes * 2 * part * len(TAPS)
    return pl.pallas_call(
        functools.partial(forward_kernel, blocks, last),
        out_shape=out_shape,
        grid_spec=pltpu.PrefetchScalarGridSpec(
            num_scalar_prefetch=1,
            grid=(len(TAPS),),
            in_specs=in_specs,
            out_specs=out_specs,
            scratch_shapes=scratch,
        ),
        compiler_params=pltpu.CompilerParams(
            dimension_semantics=("arbitrary",), vmem_limit_bytes=VMEM_LIMIT
        ),
        cost_estimate=pl.CostEstimate(
            flops=flops, transcendentals=0, bytes_accessed=blocks * (cells + 18 * part) * lanes * 2
        ),
        name="forward_last" if last else "forward_first",
    )(q, *args)


def input_grad_kernel(blocks, q_ref, g9_own, g9_sib, *refs):
    wo, ws, outs = refs[:blocks], refs[blocks : 2 * blocks], refs[2 * blocks :]
    for w0, w1, out in zip(wo, ws, outs):
        total = jnp.dot(g9_own[...], w0[...], preferred_element_type=F32)
        total += jnp.dot(g9_sib[...], w1[...], preferred_element_type=F32)
        out[...] = total.astype(out.dtype)


def input_grad_call(q, ids, dtype, g9_own, g9_sib, w_own, w_sib, lanes):
    blocks = len(ids)
    cells, depth = g9_own.shape
    w_own = w_own.reshape(depth, -1)
    w_sib = w_sib.reshape(depth, -1)
    whole = lambda shape: pl.BlockSpec(shape, lambda k, q: (0,) * len(shape))
    w_specs = [pl.BlockSpec((depth, lanes), functools.partial(lambda n, k, q: (0, q[n]), n)) for n in ids]
    return pl.pallas_call(
        functools.partial(input_grad_kernel, blocks),
        out_shape=[jax.ShapeDtypeStruct((cells, lanes), dtype)] * blocks,
        grid_spec=pltpu.PrefetchScalarGridSpec(
            num_scalar_prefetch=1,
            grid=(1,),
            in_specs=[whole(g9_own.shape), whole(g9_sib.shape)] + w_specs + w_specs,
            out_specs=[whole((cells, lanes))] * blocks,
        ),
        compiler_params=pltpu.CompilerParams(vmem_limit_bytes=VMEM_LIMIT),
        cost_estimate=pl.CostEstimate(
            flops=4 * blocks * cells * depth * lanes,
            transcendentals=0,
            bytes_accessed=4 * depth * (cells + blocks * lanes),
        ),
        name="input_grad",
    )(q, g9_own, g9_sib, *([w_own] * blocks), *([w_sib] * blocks))


def displaced_kernel(scale, *refs):
    gs = refs[:-4]
    ij, out, bias_out, field = refs[-4:]
    cells = out.shape[1]
    part = out.shape[0] // len(TAPS)
    field[0:PAD, :] = jnp.zeros((PAD, part), F32)
    field[PAD + cells : PAD + cells + PAD, :] = jnp.zeros((PAD, part), F32)
    at = PAD
    for g in gs:
        field[at : at + g.shape[0], :] = g[...].astype(F32)
        at += g.shape[0]
    bias_out[...] = jnp.sum(field[PAD : PAD + cells, :], axis=0, keepdims=True) * scale
    i, j = ij[0], ij[1]
    for t, (a, b) in enumerate(TAPS):
        start = PAD - a * GRID - b
        moved = field[start : start + cells, :]
        keep = inside(i, j, -a, -b)
        if keep is not None:
            moved = jnp.where(keep[:, :part], moved, 0.0)
        out[t * part : (t + 1) * part, :] = jnp.transpose(moved.astype(BF16))


def displaced_call(gs, ij, scale):
    cells = sum(g.shape[0] for g in gs)
    part = gs[0].shape[1]
    return pl.pallas_call(
        functools.partial(displaced_kernel, scale),
        out_shape=[
            jax.ShapeDtypeStruct((len(TAPS) * part, cells), BF16),
            jax.ShapeDtypeStruct((1, part), F32),
        ],
        scratch_shapes=[pltpu.VMEM((cells + 2 * PAD, part), F32)],
        compiler_params=pltpu.CompilerParams(vmem_limit_bytes=VMEM_LIMIT),
        name="displaced",
    )(*gs, ij)


def weight_grad_kernel(blocks, pieces, scale, q_ref, g9t, *refs):
    xs = refs[: blocks * pieces]
    out = refs[-2]
    stack = refs[-1]
    n = pl.program_id(0)
    for m in range(blocks):

        @pl.when(n == m)
        def _(m=m):
            at = 0
            for x in xs[m * pieces : (m + 1) * pieces]:
                stack[at : at + x.shape[0], :] = x[...]
                at += x.shape[0]

    out[...] = jnp.dot(g9t[...], stack[...], preferred_element_type=F32) * scale


def weight_grad_call(q, ids, g9t, xs, total, scale, channels):
    blocks = len(ids)
    pieces = len(xs[0])
    rows, cells = g9t.shape
    part, lanes = xs[0][0].shape
    whole = lambda shape: pl.BlockSpec(shape, lambda k, q: (0,) * len(shape))
    flat = [x for group in xs for x in group]
    first = ids[0]
    aliased = [] if total is None else [total]
    return pl.pallas_call(
        functools.partial(weight_grad_kernel, blocks, pieces, scale),
        out_shape=jax.ShapeDtypeStruct((rows, channels), F32),
        grid_spec=pltpu.PrefetchScalarGridSpec(
            num_scalar_prefetch=1,
            grid=(blocks,),
            in_specs=[whole((rows, cells))]
            + [whole((part, lanes))] * len(flat)
            + [pl.BlockSpec(memory_space=pl.ANY)] * len(aliased),
            out_specs=pl.BlockSpec((rows, lanes), lambda k, q: (0, q[first + k])),
            scratch_shapes=[pltpu.VMEM((part * pieces, lanes), BF16)],
        ),
        input_output_aliases={2 + len(flat): 0} if aliased else {},
        compiler_params=pltpu.CompilerParams(
            dimension_semantics=("arbitrary",), vmem_limit_bytes=VMEM_LIMIT
        ),
        cost_estimate=pl.CostEstimate(
            flops=2 * blocks * rows * cells * lanes,
            transcendentals=0,
            bytes_accessed=2 * rows * cells + blocks * (2 * cells * lanes + 4 * rows * lanes),
        ),
        name="weight_grad",
    )(q, g9t, *flat, *aliased)


def body(inputs, weight, bias_vector, cotangent):
    part, cells = inputs.shape
    devices = lax.axis_size("filt")
    case_rows = lax.axis_size("case")
    channels = part * devices
    chips = devices // 2
    half = cells // 2
    lanes = 2 * part
    scale = 1.0 / (cells // (GRID * GRID) * case_rows)

    cycle = chip_cycle(chips)
    offsets = [0]
    for d in range(1, chips // 2):
        offsets += [-d, d]
    offsets.append(-(chips // 2))
    slot = {d: n for n, d in enumerate(offsets)}
    slot[chips // 2] = slot[-(chips // 2)]
    place = {chip: n for n, chip in enumerate(cycle)}
    table = np.array(
        [[cycle[(place[chip] + d) % chips] for d in offsets] for chip in range(chips)], np.int32
    )
    me = lax.axis_index("filt")
    core = me % 2
    q = jnp.asarray(table)[me // 2]

    forwards, backwards = [], []
    for n, chip in enumerate(cycle):
        for c in range(2):
            forwards.append((2 * chip + c, 2 * cycle[(n + 1) % chips] + c))
            backwards.append((2 * chip + c, 2 * cycle[(n - 1) % chips] + c))
    swap = [(n, n ^ 1) for n in range(devices)]
    onward = lambda v: lax.ppermute(v, "filt", forwards)
    back = lambda v: lax.ppermute(v, "filt", backwards)
    sibling = lambda v: lax.ppermute(v, "filt", swap)

    x_t = jnp.transpose(inputs)
    mine = lax.dynamic_slice_in_dim(x_t, core * half, half, 0)
    theirs = sibling(lax.dynamic_slice_in_dim(x_t, (1 - core) * half, half, 0))
    own_block = jnp.where(
        core == 0,
        jnp.concatenate([mine, theirs], axis=1),
        jnp.concatenate([theirs, mine], axis=1),
    )
    w_own, w_sib = weight, sibling(weight)
    cot_t = jnp.transpose(cotangent)
    cot_own = lax.dynamic_slice_in_dim(cot_t, core * half, half, 0)
    cot_sib = sibling(lax.dynamic_slice_in_dim(cot_t, (1 - core) * half, half, 0))
    bias_row = bias_vector[None, :]
    bias_row = jnp.concatenate([bias_row, sibling(bias_row)], axis=1)

    block = {0: own_block}
    for s in range(1, chips // 2 + 1):
        block[-s] = onward(block[-s + 1])
        if s < chips // 2:
            block[s] = back(block[s - 1])

    position = np.arange(half) % (GRID * GRID)
    ij_half = np.stack([position // GRID, position % GRID]).astype(np.int32)
    width = max(part, 128)
    spread = lambda v: jnp.broadcast_to(jnp.asarray(v)[:, :, None], v.shape + (width,))
    ij = spread(ij_half)
    early = 2 * (chips // 4) + 1
    ids = list(range(chips))
    arrived = [block[d] for d in offsets]
    carry = forward_call(q, ids[:early], arrived[:early], w_own, w_sib, ij)
    act_own, act_sib, g_own, g_sib, g9_own, g9_sib = forward_call(
        q, ids[early:], arrived[early:], w_own, w_sib, ij, (carry, bias_row, cot_own, cot_sib)
    )

    grad_at = lambda ds, dtype: dict(
        zip(ds, input_grad_call(q, [slot[d] for d in ds], dtype, g9_own, g9_sib, w_own, w_sib, lanes))
    )
    far = chips // 2
    product = grad_at([far, -(far - 1)], BF16)
    for s in range(1, far):
        ds = [far - s] + ([-(far - 1 - s)] if far - 1 - s > 0 else [])
        product.update(grad_at(ds, F32))
    product.update(grad_at([0], F32))
    ahead = onward(product[far])
    behind = back(product[-(far - 1)])
    for s in range(1, far):
        ahead = onward((product[far - s] + ahead.astype(F32)).astype(BF16))
        d = far - 1 - s
        if d > 0:
            behind = back((product[-d] + behind.astype(F32)).astype(BF16))
    final = (product[0] + ahead.astype(F32) + behind.astype(F32)).astype(BF16)
    keep = lax.dynamic_slice_in_dim(final, core * part, part, 1)
    other = sibling(lax.dynamic_slice_in_dim(final, (1 - core) * part, part, 1))
    join = lambda a, b: jnp.transpose(
        jnp.where(core == 0, jnp.concatenate([a, b], axis=0), jnp.concatenate([b, a], axis=0))
    )
    input_grad = join(keep, other)
    activated = join(act_own, sibling(act_sib))

    pair = case_rows == 2
    across = lambda v: lax.ppermute(v, "case", [(0, 1), (1, 0)])
    gs = [g_own, sibling(g_sib)]
    groups = []
    for x in arrived:
        group = [x, sibling(x)]
        if pair:
            far_x = across(x)
            group += [far_x, sibling(far_x)]
        groups.append(group)
    if pair:
        gs += [across(g) for g in gs]
    ij_all = spread(np.tile(ij_half, (1, len(gs))))
    g9t, bias_grad = displaced_call(gs, ij_all, scale)
    total = None
    step = 4
    for n in range(0, chips, step):
        total = weight_grad_call(
            q, ids[n : n + step], g9t, groups[n : n + step], total, scale, channels
        )
    bias_grad = bias_grad[0]
    if not pair:
        total, bias_grad = lax.psum((total, bias_grad), "case")
    weight_grad = total.reshape(len(TAPS), part, channels)
    return activated, input_grad, weight_grad, bias_grad


def solution(mesh):
    in_specs = (P("filt", "case"), P(None, "filt", None), P("filt"), P("filt", "case"))
    out_specs = (P("filt", "case"), P("filt", "case"), P(None, "filt", None), P("filt"))
    return jax.shard_map(body, mesh=mesh, in_specs=in_specs, out_specs=out_specs, check_vma=False)
```

```python
import functools

import jax
import jax.numpy as jnp
import numpy as np
from jax import lax
from jax.experimental import pallas as pl
from jax.experimental.pallas import tpu as pltpu
from jax.sharding import PartitionSpec as P

GRID = 24
FIELD = GRID * GRID
STEPS = (-1, 0, 1)
EDGE = 8
F32 = jnp.float32
BF16 = jnp.bfloat16
MIB = 1024 * 1024
VMEM = pl.BlockSpec(memory_space=pltpu.VMEM)
SMEM = pl.BlockSpec(memory_space=pltpu.SMEM)


def chip_cycle(chips):
    rows = 4
    cols = chips // rows
    walk = [(r, 0) for r in range(rows)]
    for r in reversed(range(rows)):
        across = range(1, cols) if (rows - 1 - r) % 2 == 0 else reversed(range(1, cols))
        walk += [(r, c) for c in across]
    return [r * cols + c for r, c in walk]


def rows_moved(v, a):
    if a == 0:
        return v
    gap = jnp.zeros((GRID, v.shape[1]), v.dtype)
    pieces = []
    for s in range(0, v.shape[0], FIELD):
        pieces += [v[s + GRID : s + FIELD], gap] if a > 0 else [gap, v[s : s + FIELD - GRID]]
    return jnp.concatenate(pieces, axis=0)


def grid_columns(cells, lanes):
    r = lax.broadcasted_iota(jnp.int32, (cells, lanes), 0)
    return lax.rem(r, GRID)


def columns_moved(field, v, b, col):
    if b == 0:
        return v
    cells, lanes = v.shape
    field[EDGE : EDGE + cells, :lanes] = v
    moved = field[EDGE + b : EDGE + b + cells, :lanes]
    ok = col >= 1 if b < 0 else col < GRID - 1
    return jnp.where(ok, moved, 0.0)


def clear_edges(field):
    rows, lanes = field.shape
    field[0:EDGE, :] = jnp.zeros((EDGE, lanes), field.dtype)
    field[rows - EDGE : rows, :] = jnp.zeros((EDGE, lanes), field.dtype)


def forward_sums(q_ref, slots, xs, w_own, w_sib, carry, b):
    lanes = xs[0][0].shape[1] if isinstance(xs[0], (list, tuple)) else xs[0].shape[1]
    total = None if carry is None else carry
    for a in STEPS:
        tap = (a + 1) * 3 + b + 1
        part = None
        for n, x in zip(slots, xs):
            cols = pl.ds(pl.multiple_of(q_ref[n] * lanes, lanes), lanes)
            w = jnp.concatenate([w_own[tap, :, cols], w_sib[tap, :, cols]], axis=0)
            v = jnp.concatenate([p[...] for p in x], axis=0) if isinstance(x, (list, tuple)) else x[...]
            y = lax.dot_general(v, w, (((1,), (1,)), ((), ())), preferred_element_type=F32)
            part = y if part is None else part + y
        part = rows_moved(part, a)
        total = part if total is None else total + part
    return total


def forward_kernel(slots, has_carry, q_ref, w_own, w_sib, *refs):
    refs = list(refs)
    carry = refs.pop(0) if has_carry else None
    xs, out = refs[:-1], refs[-1]
    for b in STEPS:
        before = carry[b + 1] if has_carry else None
        out[b + 1] = forward_sums(q_ref, slots, xs, w_own, w_sib, before, b)


def forward_call(q, slots, xs, w_own, w_sib, carry):
    cells, lanes = xs[0].shape
    outs = 2 * w_own.shape[1]
    args = ([] if carry is None else [carry]) + list(xs)
    return pl.pallas_call(
        functools.partial(forward_kernel, slots, carry is not None),
        out_shape=jax.ShapeDtypeStruct((3, cells, outs), F32),
        in_specs=[SMEM] + [VMEM] * (2 + len(args)),
        out_specs=VMEM,
        compiler_params=pltpu.CompilerParams(vmem_limit_bytes=8 * MIB),
        cost_estimate=pl.CostEstimate(
            flops=18 * len(xs) * cells * lanes * outs, transcendentals=0, bytes_accessed=8 * MIB
        ),
        name="forward",
    )(q, w_own, w_sib, *args)


def gate_kernel(slots, halves, q_ref, w_own, w_sib, carry, bias, cot_own, cot_sib, *refs):
    xs = refs[: len(slots) * halves]
    act_own, act_sib, g_own, g_sib, g9, field = refs[len(slots) * halves :]
    xs = [xs[n : n + halves] for n in range(0, len(xs), halves)]
    cells = act_own.shape[0]
    part = act_own.shape[1]
    lanes = 2 * part
    col = grid_columns(cells, lanes)
    clear_edges(field)
    preact = bias[0:1, :]
    for b in (0, -1, 1):
        sums = forward_sums(q_ref, slots, xs, w_own, w_sib, carry[b + 1], b)
        preact = preact + columns_moved(field, sums, b, col)
    gate = jax.nn.sigmoid(preact)
    act = (preact * gate).astype(BF16)
    act_own[...], act_sib[...] = act[:, :part], act[:, part:]
    cot = jnp.concatenate([cot_own[...], cot_sib[...]], axis=1).astype(F32)
    grad = (cot * gate * (1.0 + preact * (1.0 - gate))).astype(BF16)
    g_own[...], g_sib[...] = grad[:, :part], grad[:, part:]
    grad = grad.astype(F32)
    for b in STEPS:
        side = columns_moved(field, grad, -b, col)
        for a in STEPS:
            tap = (a + 1) * 3 + b + 1
            g9[:, tap * lanes : (tap + 1) * lanes] = rows_moved(side, -a).astype(BF16)


def gate_call(q, slots, xs, w_own, w_sib, carry, bias, cot_own, cot_sib):
    cells = carry.shape[1]
    outs = carry.shape[2]
    part = outs // 2
    halves = len(xs[0])
    flat = [p for x in xs for p in x]
    piece = jax.ShapeDtypeStruct((cells, part), BF16)
    return pl.pallas_call(
        functools.partial(gate_kernel, slots, halves),
        out_shape=[piece] * 4 + [jax.ShapeDtypeStruct((cells, 9 * outs), BF16)],
        in_specs=[SMEM] + [VMEM] * (6 + len(flat)),
        out_specs=[VMEM] * 5,
        scratch_shapes=[pltpu.VMEM((cells + 2 * EDGE, outs), F32)],
        compiler_params=pltpu.CompilerParams(vmem_limit_bytes=10 * MIB),
        cost_estimate=pl.CostEstimate(
            flops=18 * len(xs) * cells * flat[0].shape[1] * outs,
            transcendentals=cells * outs,
            bytes_accessed=8 * MIB,
        ),
        name="gate",
    )(q, w_own, w_sib, carry, bias, cot_own, cot_sib, *flat)


def input_grad_kernel(slots, pieces, q_ref, w_own, w_sib, g9, *outs):
    lanes = outs[0].shape[1]
    outs = list(outs)
    for n in slots:
        cols = pl.ds(pl.multiple_of(q_ref[n] * lanes, lanes), lanes)
        w = jnp.concatenate([w[tap, :, cols] for tap in range(9) for w in (w_own, w_sib)], axis=0)
        total = jnp.dot(g9[...], w, preferred_element_type=F32)
        rows = total.shape[0] // pieces
        for p in range(pieces):
            out = outs.pop(0)
            out[...] = total[p * rows : (p + 1) * rows].astype(out.dtype)


def input_grad_call(q, slots, dtype, pieces, g9, w_own, w_sib, lanes):
    cells, depth = g9.shape
    count = len(slots) * pieces
    return pl.pallas_call(
        functools.partial(input_grad_kernel, slots, pieces),
        out_shape=[jax.ShapeDtypeStruct((cells // pieces, lanes), dtype)] * count,
        in_specs=[SMEM] + [VMEM] * 3,
        out_specs=[VMEM] * count,
        compiler_params=pltpu.CompilerParams(vmem_limit_bytes=8 * MIB),
        cost_estimate=pl.CostEstimate(
            flops=2 * len(slots) * cells * depth * lanes, transcendentals=0, bytes_accessed=8 * MIB
        ),
        name="input_grad",
    )(q, w_own, w_sib, g9)


def displaced_kernel(scale, *refs):
    gs = refs[:-3]
    out, bias_out, field = refs[-3:]
    cells = out.shape[1]
    part = out.shape[0] // 9
    clear_edges(field)
    grad = jnp.concatenate([g[...] for g in gs], axis=0).astype(F32)
    bias_out[...] = jnp.sum(grad, axis=0, keepdims=True) * scale
    col = grid_columns(cells, part)
    for b in STEPS:
        side = columns_moved(field, grad, -b, col)
        for a in STEPS:
            tap = (a + 1) * 3 + b + 1
            moved = rows_moved(side, -a).astype(BF16)
            out[tap * part : (tap + 1) * part, :] = jnp.transpose(moved)


def displaced_call(gs, scale):
    cells = sum(g.shape[0] for g in gs)
    part = gs[0].shape[1]
    return pl.pallas_call(
        functools.partial(displaced_kernel, scale),
        out_shape=[
            jax.ShapeDtypeStruct((9 * part, cells), BF16),
            jax.ShapeDtypeStruct((1, part), F32),
        ],
        in_specs=[VMEM] * len(gs),
        out_specs=[VMEM] * 2,
        scratch_shapes=[pltpu.VMEM((cells + 2 * EDGE, part), F32)],
        compiler_params=pltpu.CompilerParams(vmem_limit_bytes=16 * MIB),
        cost_estimate=pl.CostEstimate(flops=9 * cells * part, transcendentals=0, bytes_accessed=8 * MIB),
        name="displaced",
    )(*gs)


def weight_grad_kernel(blocks, pieces, scale, q_ref, g9t, *refs):
    xs, out = refs[: blocks * pieces], refs[-1]
    for m in range(blocks):

        @pl.when(pl.program_id(0) == m)
        def _(m=m):
            x = jnp.concatenate([x[...] for x in xs[m * pieces : (m + 1) * pieces]], axis=0)
            out[...] = jnp.dot(g9t[...], x, preferred_element_type=F32) * scale


def weight_grad_call(q, slots, g9t, xs, total, scale, channels):
    blocks = len(slots)
    pieces = len(xs[0])
    rows, cells = g9t.shape
    lanes = xs[0][0].shape[1]
    flat = [x for group in xs for x in group]
    first = slots[0]
    aliased = [] if total is None else [total]
    return pl.pallas_call(
        functools.partial(weight_grad_kernel, blocks, pieces, scale),
        out_shape=jax.ShapeDtypeStruct((rows, channels), F32),
        grid_spec=pltpu.PrefetchScalarGridSpec(
            num_scalar_prefetch=1,
            grid=(blocks,),
            in_specs=[VMEM] * (1 + len(flat)) + [pl.BlockSpec(memory_space=pl.ANY)] * len(aliased),
            out_specs=pl.BlockSpec((rows, lanes), lambda k, q: (0, q[first + k])),
        ),
        input_output_aliases={2 + len(flat): 0} if aliased else {},
        compiler_params=pltpu.CompilerParams(
            dimension_semantics=("arbitrary",), vmem_limit_bytes=12 * MIB
        ),
        cost_estimate=pl.CostEstimate(
            flops=2 * blocks * rows * cells * lanes,
            transcendentals=0,
            bytes_accessed=2 * rows * cells + blocks * (2 * cells * lanes + 4 * rows * lanes),
        ),
        name="weight_grad",
    )(q, g9t, *flat, *aliased)


def body(inputs, weight, bias_vector, cotangent):
    part, cells = inputs.shape
    devices = lax.axis_size("filt")
    case_rows = lax.axis_size("case")
    channels = part * devices
    chips = devices // 2
    half = cells // 2
    lanes = 2 * part
    far = chips // 2
    scale = 1.0 / (cells // FIELD * case_rows)

    cycle = chip_cycle(chips)
    offsets = [0]
    for d in range(1, far):
        offsets += [-d, d]
    offsets.append(far)
    slot = {d: n for n, d in enumerate(offsets)}
    place = {chip: n for n, chip in enumerate(cycle)}
    table = np.array(
        [[cycle[(place[chip] + d) % chips] for d in offsets] for chip in range(chips)], np.int32
    )
    me = lax.axis_index("filt")
    core = me % 2
    q = lax.dynamic_index_in_dim(jnp.asarray(table), me // 2, 0, keepdims=False)

    forwards, backwards = [], []
    for n, chip in enumerate(cycle):
        for c in range(2):
            forwards.append((2 * chip + c, 2 * cycle[(n + 1) % chips] + c))
            backwards.append((2 * chip + c, 2 * cycle[(n - 1) % chips] + c))
    swap = [(n, n ^ 1) for n in range(devices)]
    onward = lambda v: lax.ppermute(v, "filt", forwards)
    back = lambda v: lax.ppermute(v, "filt", backwards)
    sibling = lambda v: lax.ppermute(v, "filt", swap)
    pair = case_rows == 2
    across = lambda v: lax.ppermute(v, "case", [(0, 1), (1, 0)])
    tie = lambda *v: lax.optimization_barrier(v)

    x_t = jnp.transpose(inputs)
    mine = lax.dynamic_slice_in_dim(x_t, core * half, half, 0)
    theirs = sibling(lax.dynamic_slice_in_dim(x_t, (1 - core) * half, half, 0))
    own_block = jnp.where(
        core == 0,
        jnp.concatenate([mine, theirs], axis=1),
        jnp.concatenate([theirs, mine], axis=1),
    )
    block = {0: own_block, -1: onward(own_block), 1: back(own_block)}
    theirs, weight, cotangent, bias_vector = tie(theirs, weight, cotangent, bias_vector)
    w_own, w_sib = weight, sibling(weight)
    cot_t = jnp.transpose(cotangent)
    cot_own = lax.dynamic_slice_in_dim(cot_t, core * half, half, 0)
    cot_sib = sibling(lax.dynamic_slice_in_dim(cot_t, (1 - core) * half, half, 0))
    bias_row = bias_vector[None, :]
    bias_row = jnp.concatenate([bias_row, sibling(bias_row)], axis=1)

    carry = forward_call(q, [0, 1, 2], [block[d] for d in (0, -1, 1)], w_own, w_sib, None)
    for s in range(2, far):
        block[-s], block[s] = onward(block[-s + 1]), back(block[s - 1])
        block[-s], block[s], carry = tie(block[-s], block[s], carry)
        if s < far - 1:
            carry = forward_call(q, [slot[-s], slot[s]], [block[-s], block[s]], w_own, w_sib, carry)
    s = far - 1
    top, low = onward(block[-s][: half // 2]), back(block[s][half // 2 :])
    carry = forward_call(q, [slot[-s], slot[s]], [block[-s], block[s]], w_own, w_sib, carry)
    top, low, carry = tie(top, low, carry)
    act_own, act_sib, g_own, g_sib, g9 = gate_call(
        q, [slot[far]], [[top, low]], w_own, w_sib, carry, bias_row, cot_own, cot_sib
    )

    grad_at = lambda ds, dtype, pieces=1: input_grad_call(
        q, [slot[d] for d in ds], dtype, pieces, g9, w_own, w_sib, lanes
    )
    top_p, low_p = grad_at([far], BF16, 2)
    ahead, behind = onward(top_p), back(low_p)
    p_ahead, p_behind = grad_at([far - 1, -(far - 1)], F32)
    rest_ds = [d for n in range(far - 2, 0, -1) for d in (n, -n)] + [0]
    ahead, behind, p_ahead, p_behind, g9 = tie(ahead, behind, p_ahead, p_behind, g9)
    rest = dict(zip(rest_ds, grad_at(rest_ds, F32)))
    hop = half // 2
    ahead = jnp.concatenate([p_ahead[:hop] + ahead.astype(F32), p_ahead[hop:]], axis=0)
    behind = jnp.concatenate([p_behind[:hop], p_behind[hop:] + behind.astype(F32)], axis=0)
    ahead, behind = onward(ahead.astype(BF16)), back(behind.astype(BF16))
    for s in range(far - 2, 0, -1):
        ahead = onward((rest[s] + ahead.astype(F32)).astype(BF16))
        behind = back((rest[-s] + behind.astype(F32)).astype(BF16))
    final = (rest[0] + ahead.astype(F32) + behind.astype(F32)).astype(BF16)
    keep = lax.dynamic_slice_in_dim(final, core * part, part, 1)
    other = sibling(lax.dynamic_slice_in_dim(final, (1 - core) * part, part, 1))
    join = lambda a, b: jnp.transpose(
        jnp.where(core == 0, jnp.concatenate([a, b], axis=0), jnp.concatenate([b, a], axis=0))
    )
    input_grad = join(keep, other)
    activated = join(act_own, sibling(act_sib))

    block[far] = jnp.concatenate([top, low], axis=0)
    gs = [g_own, sibling(g_sib)]
    groups = []
    for d in offsets:
        group = [block[d], sibling(block[d])]
        if pair:
            far_x = across(block[d])
            group += [far_x, sibling(far_x)]
        groups.append(group)
    if pair:
        gs += [across(g) for g in gs]
    g9t, bias_grad = displaced_call(gs, scale)
    total = None
    step = chips // 4
    for n in range(0, chips, step):
        ids = list(range(n, n + step))
        total = weight_grad_call(q, ids, g9t, [groups[i] for i in ids], total, scale, channels)
    bias_grad = bias_grad[0]
    if not pair:
        total, bias_grad = lax.psum((total, bias_grad), "case")
    weight_grad = total.reshape(9, part, channels)
    return activated, input_grad, weight_grad, bias_grad


def solution(mesh):
    in_specs = (P("filt", "case"), P(None, "filt", None), P("filt"), P("filt", "case"))
    out_specs = (P("filt", "case"), P("filt", "case"), P(None, "filt", None), P("filt"))
    return jax.shard_map(body, mesh=mesh, in_specs=in_specs, out_specs=out_specs, check_vma=False)
```

```python
import functools

import jax
import jax.numpy as jnp
import numpy as np
from jax import lax
from jax.experimental import pallas as pl
from jax.experimental.pallas import tpu as pltpu
from jax.sharding import PartitionSpec as P

GRID = 24
FIELD = GRID * GRID
STEPS = (-1, 0, 1)
EDGE = 8
F32 = jnp.float32
BF16 = jnp.bfloat16
MIB = 1024 * 1024
LIGHT = pl.CostEstimate(flops=1000, transcendentals=0, bytes_accessed=1000)
VMEM = pl.BlockSpec(memory_space=pltpu.VMEM)
SMEM = pl.BlockSpec(memory_space=pltpu.SMEM)
ANY = pl.BlockSpec(memory_space=pl.ANY)
TOKEN = jax.ShapeDtypeStruct((8, 128), F32)


def chip_cycle(chips):
    rows = 4
    cols = chips // rows
    walk = [(r, 0) for r in range(rows)]
    for r in reversed(range(rows)):
        across = range(1, cols) if (rows - 1 - r) % 2 == 0 else reversed(range(1, cols))
        walk += [(r, c) for c in across]
    return [r * cols + c for r, c in walk]


def rows_moved(v, a):
    if a == 0:
        return v
    gap = jnp.zeros((GRID, v.shape[1]), v.dtype)
    pieces = []
    for s in range(0, v.shape[0], FIELD):
        pieces += [v[s + GRID : s + FIELD], gap] if a > 0 else [gap, v[s : s + FIELD - GRID]]
    return jnp.concatenate(pieces, axis=0)


def grid_columns(cells, lanes):
    r = lax.broadcasted_iota(jnp.int32, (cells, lanes), 0)
    return lax.rem(r, GRID)


def columns_moved(field, v, b, col):
    if b == 0:
        return v
    cells, lanes = v.shape
    field[EDGE : EDGE + cells, :lanes] = v
    moved = field[EDGE + b : EDGE + b + cells, :lanes]
    ok = col >= 1 if b < 0 else col < GRID - 1
    return jnp.where(ok, moved, 0.0)


def clear_edges(field):
    rows, lanes = field.shape
    field[0:EDGE, :] = jnp.zeros((EDGE, lanes), field.dtype)
    field[rows - EDGE : rows, :] = jnp.zeros((EDGE, lanes), field.dtype)


def hold_kernel(w_own, w_sib, out, token, sems):
    part = w_own.shape[1]
    token[...] = jnp.zeros(token.shape, F32)
    copies = [
        pltpu.make_async_copy(w, out.at[:, n * part : (n + 1) * part], sems.at[n])
        for n, w in enumerate((w_own, w_sib))
    ]
    for copy in copies:
        copy.start()
    for copy in copies:
        copy.wait()


def hold_call(w_own, w_sib):
    taps, part, channels = w_own.shape
    return pl.pallas_call(
        hold_kernel,
        out_shape=[jax.ShapeDtypeStruct((taps, 2 * part, channels), BF16), TOKEN],
        in_specs=[pl.BlockSpec(memory_space=pltpu.HBM)] * 2,
        out_specs=[VMEM] * 2,
        scratch_shapes=[pltpu.SemaphoreType.DMA((2,))],
        compiler_params=pltpu.CompilerParams(vmem_limit_bytes=12 * MIB),
        cost_estimate=LIGHT,
        name="hold",
    )(w_own, w_sib)


def forward_sums(q_ref, slots, xs, w_all, carry, b):
    lanes = xs[0][0].shape[1] if isinstance(xs[0], (list, tuple)) else xs[0].shape[1]
    total = None if carry is None else carry
    for a in STEPS:
        tap = (a + 1) * 3 + b + 1
        part = None
        for n, x in zip(slots, xs):
            cols = pl.ds(pl.multiple_of(q_ref[n] * lanes, lanes), lanes)
            w = w_all[tap, :, cols]
            v = jnp.concatenate([p[...] for p in x], axis=0) if isinstance(x, (list, tuple)) else x[...]
            y = lax.dot_general(v, w, (((1,), (1,)), ((), ())), preferred_element_type=F32)
            part = y if part is None else part + y
        part = rows_moved(part, a)
        total = part if total is None else total + part
    return total


def forward_kernel(slots, has_carry, q_ref, after, w_all, *refs):
    refs = list(refs)
    carry = refs.pop(0) if has_carry else None
    xs, out, token = refs[:-2], refs[-2], refs[-1]
    token[...] = jnp.zeros(token.shape, F32)
    for b in STEPS:
        before = carry[b + 1] if has_carry else None
        out[b + 1] = forward_sums(q_ref, slots, xs, w_all, before, b)


def forward_call(q, after, slots, xs, w_all, carry):
    cells, lanes = xs[0].shape
    outs = w_all.shape[1]
    args = ([] if carry is None else [carry]) + list(xs)
    return pl.pallas_call(
        functools.partial(forward_kernel, slots, carry is not None),
        out_shape=[jax.ShapeDtypeStruct((3, cells, outs), F32), TOKEN],
        in_specs=[SMEM, ANY] + [VMEM] * (1 + len(args)),
        out_specs=[VMEM] * 2,
        compiler_params=pltpu.CompilerParams(vmem_limit_bytes=8 * MIB),
        cost_estimate=LIGHT,
        name="forward",
    )(q, after, w_all, *args)


def gate_kernel(slots, halves, q_ref, after, w_all, carry, bias, cot_own, cot_sib, *refs):
    xs = refs[: len(slots) * halves]
    act_own, act_sib, g_own, g_sib, g9, field = refs[len(slots) * halves :]
    xs = [xs[n : n + halves] for n in range(0, len(xs), halves)]
    cells = act_own.shape[0]
    part = act_own.shape[1]
    lanes = 2 * part
    col = grid_columns(cells, lanes)
    clear_edges(field)
    preact = bias[0:1, :]
    for b in (0, -1, 1):
        sums = forward_sums(q_ref, slots, xs, w_all, carry[b + 1], b)
        preact = preact + columns_moved(field, sums, b, col)
    gate = jax.nn.sigmoid(preact)
    act = (preact * gate).astype(BF16)
    act_own[...], act_sib[...] = act[:, :part], act[:, part:]
    cot = jnp.concatenate([cot_own[...], cot_sib[...]], axis=1).astype(F32)
    grad = (cot * gate * (1.0 + preact * (1.0 - gate))).astype(BF16)
    g_own[...], g_sib[...] = grad[:, :part], grad[:, part:]
    grad = grad.astype(F32)
    for b in STEPS:
        side = columns_moved(field, grad, -b, col)
        for a in STEPS:
            tap = (a + 1) * 3 + b + 1
            g9[:, tap * lanes : (tap + 1) * lanes] = rows_moved(side, -a).astype(BF16)


def gate_call(q, after, slots, xs, w_all, carry, bias, cot_own, cot_sib):
    cells = carry.shape[1]
    outs = carry.shape[2]
    part = outs // 2
    halves = len(xs[0])
    flat = [p for x in xs for p in x]
    piece = jax.ShapeDtypeStruct((cells, part), BF16)
    return pl.pallas_call(
        functools.partial(gate_kernel, slots, halves),
        out_shape=[piece] * 4 + [jax.ShapeDtypeStruct((cells, 9 * outs), BF16)],
        in_specs=[SMEM, ANY] + [VMEM] * (5 + len(flat)),
        out_specs=[VMEM] * 5,
        scratch_shapes=[pltpu.VMEM((cells + 2 * EDGE, outs), F32)],
        compiler_params=pltpu.CompilerParams(vmem_limit_bytes=10 * MIB),
        cost_estimate=LIGHT,
        name="gate",
    )(q, after, w_all, carry, bias, cot_own, cot_sib, *flat)


def input_grad_kernel(slots, pieces, q_ref, after, w_all, g9, *outs):
    lanes = outs[0].shape[1]
    outs = list(outs)
    token = outs.pop()
    token[...] = jnp.zeros(token.shape, F32)
    for n in slots:
        cols = pl.ds(pl.multiple_of(q_ref[n] * lanes, lanes), lanes)
        w = w_all[:, :, cols].reshape(-1, lanes)
        total = jnp.dot(g9[...], w, preferred_element_type=F32)
        rows = total.shape[0] // pieces
        for p in range(pieces):
            out = outs.pop(0)
            out[...] = total[p * rows : (p + 1) * rows].astype(out.dtype)


def input_grad_call(q, after, slots, dtype, pieces, g9, w_all, lanes):
    cells, depth = g9.shape
    count = len(slots) * pieces
    return pl.pallas_call(
        functools.partial(input_grad_kernel, slots, pieces),
        out_shape=[jax.ShapeDtypeStruct((cells // pieces, lanes), dtype)] * count + [TOKEN],
        in_specs=[SMEM, ANY] + [VMEM] * 2,
        out_specs=[VMEM] * (count + 1),
        compiler_params=pltpu.CompilerParams(vmem_limit_bytes=8 * MIB),
        cost_estimate=LIGHT,
        name="input_grad",
    )(q, after, w_all, g9)


def displaced_kernel(scale, core, after, act_own, act_sib, *refs):
    gs = refs[:-4]
    out, bias_out, act_out, field = refs[-4:]
    for c, order in enumerate(((act_own, act_sib), (act_sib, act_own))):

        @pl.when(core[0] == c)
        def _(order=order):
            act_out[...] = jnp.transpose(jnp.concatenate([v[...] for v in order], axis=0))

    cells = out.shape[1]
    part = out.shape[0] // 9
    clear_edges(field)
    grad = jnp.concatenate([g[...] for g in gs], axis=0).astype(F32)
    bias_out[...] = jnp.sum(grad, axis=0, keepdims=True) * scale
    col = grid_columns(cells, part)
    for b in STEPS:
        side = columns_moved(field, grad, -b, col)
        for a in STEPS:
            tap = (a + 1) * 3 + b + 1
            moved = rows_moved(side, -a).astype(BF16)
            out[tap * part : (tap + 1) * part, :] = jnp.transpose(moved)


def displaced_call(core, after, act_own, act_sib, gs, scale):
    cells = sum(g.shape[0] for g in gs)
    part = gs[0].shape[1]
    return pl.pallas_call(
        functools.partial(displaced_kernel, scale),
        out_shape=[
            jax.ShapeDtypeStruct((9 * part, cells), BF16),
            jax.ShapeDtypeStruct((1, part), F32),
            jax.ShapeDtypeStruct((part, 2 * act_own.shape[0]), BF16),
        ],
        in_specs=[SMEM, ANY] + [VMEM] * (2 + len(gs)),
        out_specs=[VMEM] * 3,
        scratch_shapes=[pltpu.VMEM((cells + 2 * EDGE, part), F32)],
        compiler_params=pltpu.CompilerParams(vmem_limit_bytes=10 * MIB),
        cost_estimate=LIGHT,
        name="displaced",
    )(core, after, act_own, act_sib, *gs)


def weight_grad_kernel(places, scale, q_ref, after, g9t, *refs):
    x = jnp.concatenate([x[...] for x in refs[:places]], axis=0)
    out, token = refs[-2:]
    token[...] = jnp.zeros(token.shape, F32)
    out[...] = jnp.dot(g9t[...], x, preferred_element_type=F32) * scale


def weight_grad_call(q, after, slots, g9t, xs, total, scale, channels):
    blocks = len(slots)
    rows, cells = g9t.shape
    lanes = xs[0].shape[1]
    first = slots[0]
    aliased = [] if total is None else [total]
    return pl.pallas_call(
        functools.partial(weight_grad_kernel, len(xs), scale),
        out_shape=[jax.ShapeDtypeStruct((rows, channels), F32), TOKEN],
        grid_spec=pltpu.PrefetchScalarGridSpec(
            num_scalar_prefetch=1,
            grid=(blocks,),
            in_specs=[ANY, VMEM]
            + [pl.BlockSpec((xs[0].shape[0] // blocks, lanes), lambda k, q: (k, 0))] * len(xs)
            + [ANY] * len(aliased),
            out_specs=[pl.BlockSpec((rows, lanes), lambda k, q: (0, q[first + k])), VMEM],
        ),
        input_output_aliases={3 + len(xs): 0} if aliased else {},
        compiler_params=pltpu.CompilerParams(
            dimension_semantics=("arbitrary",), vmem_limit_bytes=12 * MIB
        ),
        cost_estimate=LIGHT,
        name="weight_grad",
    )(q, after, g9t, *xs, *aliased)


def body(inputs, weight, bias_vector, cotangent):
    part, cells = inputs.shape
    devices = lax.axis_size("filt")
    case_rows = lax.axis_size("case")
    channels = part * devices
    chips = devices // 2
    half = cells // 2
    lanes = 2 * part
    far = chips // 2
    scale = 1.0 / (cells // FIELD * case_rows)

    cycle = chip_cycle(chips)
    offsets = [0]
    for d in range(1, far):
        offsets += [-d, d]
    offsets.append(far)
    slot = {d: n for n, d in enumerate(offsets)}
    place = {chip: n for n, chip in enumerate(cycle)}
    table = np.array(
        [[cycle[(place[chip] + d) % chips] for d in offsets] for chip in range(chips)], np.int32
    )
    me = lax.axis_index("filt")
    core = me % 2
    q = lax.dynamic_index_in_dim(jnp.asarray(table), me // 2, 0, keepdims=False)

    forwards, backwards = [], []
    for n, chip in enumerate(cycle):
        for c in range(2):
            forwards.append((2 * chip + c, 2 * cycle[(n + 1) % chips] + c))
            backwards.append((2 * chip + c, 2 * cycle[(n - 1) % chips] + c))
    swap = [(n, n ^ 1) for n in range(devices)]
    onward = lambda v: lax.ppermute(v, "filt", forwards)
    back = lambda v: lax.ppermute(v, "filt", backwards)
    sibling = lambda v: lax.ppermute(v, "filt", swap)
    pair = case_rows == 2
    across = lambda v: lax.ppermute(v, "case", [(0, 1), (1, 0)])
    tie = lambda *v: lax.optimization_barrier(v)

    x_t = jnp.transpose(inputs)
    mine = lax.dynamic_slice_in_dim(x_t, core * half, half, 0)
    theirs = sibling(lax.dynamic_slice_in_dim(x_t, (1 - core) * half, half, 0))
    own_block = jnp.where(
        core == 0,
        jnp.concatenate([mine, theirs], axis=1),
        jnp.concatenate([theirs, mine], axis=1),
    )
    block = {0: own_block, -1: onward(own_block), 1: back(own_block)}
    theirs, weight, cotangent, bias_vector = tie(theirs, weight, cotangent, bias_vector)
    w_own, w_sib = weight, sibling(weight)
    cot_t = jnp.transpose(cotangent)
    cot_own = lax.dynamic_slice_in_dim(cot_t, core * half, half, 0)
    cot_sib = sibling(lax.dynamic_slice_in_dim(cot_t, (1 - core) * half, half, 0))
    bias_row = bias_vector[None, :]
    bias_sib = sibling(bias_row)
    block[-1], block[1], cot_sib, bias_sib = tie(block[-1], block[1], cot_sib, bias_sib)
    bias_row = jnp.concatenate([bias_row, bias_sib], axis=1)

    stacks = []

    def stack(ds, parts):
        x = jnp.concatenate(parts, axis=0)
        stacks.append(([slot[d] for d in ds], x, across(x) if pair else None))

    w_all, token = hold_call(w_own, w_sib)
    for s in range(1, far):
        if s > 1:
            block[-s], block[s] = onward(block[-s + 1]), back(block[s - 1])
            if s == far - 1:
                early = offsets[: 2 * far - 3]
                carry, token = forward_call(
                    q, token, [slot[d] for d in early], [block[d] for d in early], w_all, None
                )
            block[-s], block[s], token = tie(block[-s], block[s], token)
        if s < far - 1:
            ds = [0, -1, 1] if s == 1 else [-s, s]
            stack(ds, [block[d] for d in ds])
    s = far - 1
    top, low = onward(block[-s][: half // 2]), back(block[s][half // 2 :])
    carry, token = forward_call(q, token, [slot[-s], slot[s]], [block[-s], block[s]], w_all, carry)
    tops = [top, low, token] + [x for _, _, x in stacks[:1] if pair]
    top, low, token, *done = tie(*tops)
    others = done
    act_own, act_sib, g_own, g_sib, g9 = gate_call(
        q, token, [slot[far]], [[top, low]], w_all, carry, bias_row, cot_own, cot_sib
    )

    grad_at = lambda after, ds, dtype, pieces=1: input_grad_call(
        q, after, [slot[d] for d in ds], dtype, pieces, g9, w_all, lanes
    )
    top_p, low_p, after_top = grad_at(token, [far], BF16, 2)
    ahead, behind = onward(top_p), back(low_p)
    act_recv, g_recv = sibling(act_sib), sibling(g_sib)
    p_ahead, p_behind, token = grad_at(after_top, [far - 1, -(far - 1)], F32)
    gs = [jnp.concatenate([g_own, g_recv], axis=0)]
    waits = [act_recv, gs[0]] + [x for _, _, x in stacks[1:] if pair]
    ahead, behind, token, act_recv, gs[0], *done = tie(ahead, behind, token, *waits)
    others += done
    if pair:
        gs.append(across(gs[0]))
    stack(
        [-(far - 1), far - 1, far], [block[-(far - 1)], block[far - 1], top, low]
    )
    hop = half // 2
    ahead = jnp.concatenate([p_ahead[:hop] + ahead.astype(F32), p_ahead[hop:]], axis=0)
    behind = jnp.concatenate([p_behind[:hop], p_behind[hop:] + behind.astype(F32)], axis=0)
    ahead, behind = tie(ahead.astype(BF16), behind.astype(BF16))
    ahead, behind = onward(ahead), back(behind)
    rest_ds = [d for n in range(far - 2, 0, -1) for d in (n, -n)] + [0]
    *rest, token = grad_at(token, rest_ds, F32)
    rest = dict(zip(rest_ds, rest))
    ahead, behind, token, *gs = tie(ahead, behind, token, *gs)

    g9t, bias_grad, activated = displaced_call(core[None], token, act_own, act_recv, gs, scale)
    state = {"total": None, "next": 0, "token": token}

    def weight_grads():
        n = state["next"]
        ids, x, _ = stacks[n]
        xs = [x, sibling(x)]
        if pair:
            xs += [others[n], sibling(others[n])]
        state["total"], state["token"] = weight_grad_call(
            q, state["token"], ids, g9t, xs, state["total"], scale, channels
        )
        state["next"] = n + 1
        return state["token"]

    for s in range(far - 2, 0, -1):
        ahead = (rest[s] + ahead.astype(F32)).astype(BF16)
        behind = (rest[-s] + behind.astype(F32)).astype(BF16)
        ahead, behind = tie(ahead, behind)
        ahead, behind = onward(ahead), back(behind)
        waits = [ahead, behind]
        if state["next"] < len(stacks) - 1:
            waits.append(weight_grads())
        else:
            waits.append(state["token"])
        if s == 1 and pair:
            waits.append(stacks[-1][2])
        ahead, behind, state["token"], *last = tie(*waits)
        others += last
    final = (rest[0] + ahead.astype(F32) + behind.astype(F32)).astype(BF16)
    keep = lax.dynamic_slice_in_dim(final, core * part, part, 1)
    other = sibling(lax.dynamic_slice_in_dim(final, (1 - core) * part, part, 1))
    while state["next"] < len(stacks):
        weight_grads()
    total = state["total"]
    input_grad = jnp.transpose(
        jnp.where(
            core == 0,
            jnp.concatenate([keep, other], axis=0),
            jnp.concatenate([other, keep], axis=0),
        )
    )
    bias_grad = bias_grad[0]
    if not pair:
        total, bias_grad = lax.psum((total, bias_grad), "case")
    weight_grad = total.reshape(9, part, channels)
    return activated, input_grad, weight_grad, bias_grad


def solution(mesh):
    in_specs = (P("filt", "case"), P(None, "filt", None), P("filt"), P("filt", "case"))
    out_specs = (P("filt", "case"), P("filt", "case"), P(None, "filt", None), P("filt"))
    return jax.shard_map(body, mesh=mesh, in_specs=in_specs, out_specs=out_specs, check_vma=False)
```

```python
import functools

import jax
import jax.numpy as jnp
import numpy as np
from jax import lax
from jax.experimental import pallas as pl
from jax.experimental.pallas import tpu as pltpu
from jax.sharding import PartitionSpec as P

GRID = 24
FIELD = GRID * GRID
STEPS = (-1, 0, 1)
EDGE = 8
F32 = jnp.float32
BF16 = jnp.bfloat16
MIB = 1024 * 1024
LIGHT = pl.CostEstimate(flops=1000, transcendentals=0, bytes_accessed=1000)
VMEM = pl.BlockSpec(memory_space=pltpu.VMEM)
SMEM = pl.BlockSpec(memory_space=pltpu.SMEM)
ANY = pl.BlockSpec(memory_space=pl.ANY)
TOKEN = jax.ShapeDtypeStruct((8, 128), F32)


def chip_cycle(chips):
    rows = 4
    cols = chips // rows
    walk = [(r, 0) for r in range(rows)]
    for r in reversed(range(rows)):
        across = range(1, cols) if (rows - 1 - r) % 2 == 0 else reversed(range(1, cols))
        walk += [(r, c) for c in across]
    return [r * cols + c for r, c in walk]


def rows_moved(v, a):
    if a == 0:
        return v
    gap = jnp.zeros((GRID, v.shape[1]), v.dtype)
    pieces = []
    for s in range(0, v.shape[0], FIELD):
        pieces += [v[s + GRID : s + FIELD], gap] if a > 0 else [gap, v[s : s + FIELD - GRID]]
    return jnp.concatenate(pieces, axis=0)


def grid_columns(cells, lanes):
    r = lax.broadcasted_iota(jnp.int32, (cells, lanes), 0)
    return lax.rem(r, GRID)


def columns_moved(field, v, b, col):
    if b == 0:
        return v
    cells, lanes = v.shape
    field[EDGE : EDGE + cells, :lanes] = v
    moved = field[EDGE + b : EDGE + b + cells, :lanes]
    ok = col >= 1 if b < 0 else col < GRID - 1
    return jnp.where(ok, moved, 0.0)


def clear_edges(field):
    rows, lanes = field.shape
    field[0:EDGE, :] = jnp.zeros((EDGE, lanes), field.dtype)
    field[rows - EDGE : rows, :] = jnp.zeros((EDGE, lanes), field.dtype)


def hold_kernel(w_own, w_sib, out, token, sems):
    part = w_own.shape[1]
    token[...] = jnp.zeros(token.shape, F32)
    copies = [
        pltpu.make_async_copy(w, out.at[:, n * part : (n + 1) * part], sems.at[n])
        for n, w in enumerate((w_own, w_sib))
    ]
    for copy in copies:
        copy.start()
    for copy in copies:
        copy.wait()


def hold_call(w_own, w_sib):
    taps, part, channels = w_own.shape
    return pl.pallas_call(
        hold_kernel,
        out_shape=[jax.ShapeDtypeStruct((taps, 2 * part, channels), BF16), TOKEN],
        in_specs=[pl.BlockSpec(memory_space=pltpu.HBM)] * 2,
        out_specs=[VMEM] * 2,
        scratch_shapes=[pltpu.SemaphoreType.DMA((2,))],
        compiler_params=pltpu.CompilerParams(vmem_limit_bytes=12 * MIB),
        cost_estimate=LIGHT,
        name="hold",
    )(w_own, w_sib)


def forward_sums(q_ref, slots, xs, w_all, carry, b):
    lanes = xs[0][0].shape[1] if isinstance(xs[0], (list, tuple)) else xs[0].shape[1]
    total = None if carry is None else carry
    for a in STEPS:
        tap = (a + 1) * 3 + b + 1
        part = None
        for n, x in zip(slots, xs):
            cols = pl.ds(pl.multiple_of(q_ref[n] * lanes, lanes), lanes)
            w = w_all[tap, :, cols]
            v = jnp.concatenate([p[...] for p in x], axis=0) if isinstance(x, (list, tuple)) else x[...]
            y = lax.dot_general(v, w, (((1,), (1,)), ((), ())), preferred_element_type=F32)
            part = y if part is None else part + y
        part = rows_moved(part, a)
        total = part if total is None else total + part
    return total


def forward_kernel(slots, has_carry, q_ref, after, w_all, *refs):
    refs = list(refs)
    carry = refs.pop(0) if has_carry else None
    xs, out, token = refs[:-2], refs[-2], refs[-1]
    token[...] = jnp.zeros(token.shape, F32)
    for b in STEPS:
        before = carry[b + 1] if has_carry else None
        out[b + 1] = forward_sums(q_ref, slots, xs, w_all, before, b)


def forward_call(q, after, slots, xs, w_all, carry):
    cells, lanes = xs[0].shape
    outs = w_all.shape[1]
    args = ([] if carry is None else [carry]) + list(xs)
    return pl.pallas_call(
        functools.partial(forward_kernel, slots, carry is not None),
        out_shape=[jax.ShapeDtypeStruct((3, cells, outs), F32), TOKEN],
        in_specs=[SMEM, ANY] + [VMEM] * (1 + len(args)),
        out_specs=[VMEM] * 2,
        compiler_params=pltpu.CompilerParams(vmem_limit_bytes=8 * MIB),
        cost_estimate=LIGHT,
        name="forward",
    )(q, after, w_all, *args)


def gate_kernel(slots, halves, q_ref, after, w_all, carry, bias, cot_own, cot_sib, *refs):
    xs = refs[: len(slots) * halves]
    act_own, act_sib, g_own, g_sib, g9, field = refs[len(slots) * halves :]
    xs = [xs[n : n + halves] for n in range(0, len(xs), halves)]
    cells = act_own.shape[0]
    part = act_own.shape[1]
    lanes = 2 * part
    col = grid_columns(cells, lanes)
    clear_edges(field)
    preact = bias[0:1, :]
    for b in (0, -1, 1):
        sums = forward_sums(q_ref, slots, xs, w_all, carry[b + 1], b)
        preact = preact + columns_moved(field, sums, b, col)
    gate = jax.nn.sigmoid(preact)
    act = (preact * gate).astype(BF16)
    act_own[...], act_sib[...] = act[:, :part], act[:, part:]
    cot = jnp.concatenate([cot_own[...], cot_sib[...]], axis=1).astype(F32)
    grad = (cot * gate * (1.0 + preact * (1.0 - gate))).astype(BF16)
    g_own[...], g_sib[...] = grad[:, :part], grad[:, part:]
    grad = grad.astype(F32)
    for b in STEPS:
        side = columns_moved(field, grad, -b, col)
        for a in STEPS:
            tap = (a + 1) * 3 + b + 1
            g9[:, tap * lanes : (tap + 1) * lanes] = rows_moved(side, -a).astype(BF16)


def gate_call(q, after, slots, xs, w_all, carry, bias, cot_own, cot_sib):
    cells = carry.shape[1]
    outs = carry.shape[2]
    part = outs // 2
    halves = len(xs[0])
    flat = [p for x in xs for p in x]
    piece = jax.ShapeDtypeStruct((cells, part), BF16)
    return pl.pallas_call(
        functools.partial(gate_kernel, slots, halves),
        out_shape=[piece] * 4 + [jax.ShapeDtypeStruct((cells, 9 * outs), BF16)],
        in_specs=[SMEM, ANY] + [VMEM] * (5 + len(flat)),
        out_specs=[VMEM] * 5,
        scratch_shapes=[pltpu.VMEM((cells + 2 * EDGE, outs), F32)],
        compiler_params=pltpu.CompilerParams(vmem_limit_bytes=10 * MIB),
        cost_estimate=LIGHT,
        name="gate",
    )(q, after, w_all, carry, bias, cot_own, cot_sib, *flat)


def input_grad_kernel(slots, pieces, q_ref, after, w_all, g9, *outs):
    lanes = outs[0].shape[1]
    outs = list(outs)
    token = outs.pop()
    token[...] = jnp.zeros(token.shape, F32)
    for n in slots:
        cols = pl.ds(pl.multiple_of(q_ref[n] * lanes, lanes), lanes)
        w = w_all[:, :, cols].reshape(-1, lanes)
        total = jnp.dot(g9[...], w, preferred_element_type=F32)
        rows = total.shape[0] // pieces
        for p in range(pieces):
            out = outs.pop(0)
            out[...] = total[p * rows : (p + 1) * rows].astype(out.dtype)


def input_grad_call(q, after, slots, dtype, pieces, g9, w_all, lanes):
    cells, depth = g9.shape
    count = len(slots) * pieces
    return pl.pallas_call(
        functools.partial(input_grad_kernel, slots, pieces),
        out_shape=[jax.ShapeDtypeStruct((cells // pieces, lanes), dtype)] * count + [TOKEN],
        in_specs=[SMEM, ANY] + [VMEM] * 2,
        out_specs=[VMEM] * (count + 1),
        compiler_params=pltpu.CompilerParams(vmem_limit_bytes=8 * MIB),
        cost_estimate=LIGHT,
        name="input_grad",
    )(q, after, w_all, g9)


def displaced_kernel(scale, core, after, act_own, act_sib, *refs):
    gs = refs[:-4]
    out, bias_out, act_out, field = refs[-4:]
    for c, order in enumerate(((act_own, act_sib), (act_sib, act_own))):

        @pl.when(core[0] == c)
        def _(order=order):
            act_out[...] = jnp.transpose(jnp.concatenate([v[...] for v in order], axis=0))

    cells = out.shape[1]
    part = out.shape[0] // 9
    clear_edges(field)
    grad = jnp.concatenate([g[...] for g in gs], axis=0).astype(F32)
    bias_out[...] = jnp.sum(grad, axis=0, keepdims=True) * scale
    col = grid_columns(cells, part)
    for b in STEPS:
        side = columns_moved(field, grad, -b, col)
        for a in STEPS:
            tap = (a + 1) * 3 + b + 1
            moved = rows_moved(side, -a).astype(BF16)
            out[tap * part : (tap + 1) * part, :] = jnp.transpose(moved)


def displaced_call(core, after, act_own, act_sib, gs, scale):
    cells = sum(g.shape[0] for g in gs)
    part = gs[0].shape[1]
    return pl.pallas_call(
        functools.partial(displaced_kernel, scale),
        out_shape=[
            jax.ShapeDtypeStruct((9 * part, cells), BF16),
            jax.ShapeDtypeStruct((1, part), F32),
            jax.ShapeDtypeStruct((part, 2 * act_own.shape[0]), BF16),
        ],
        in_specs=[SMEM, ANY] + [VMEM] * (2 + len(gs)),
        out_specs=[VMEM] * 3,
        scratch_shapes=[pltpu.VMEM((cells + 2 * EDGE, part), F32)],
        compiler_params=pltpu.CompilerParams(vmem_limit_bytes=10 * MIB),
        cost_estimate=LIGHT,
        name="displaced",
    )(core, after, act_own, act_sib, *gs)


def weight_grad_kernel(places, scale, q_ref, after, g9t, *refs):
    x = jnp.concatenate([x[...] for x in refs[:places]], axis=0)
    out, token = refs[-2:]
    token[...] = jnp.zeros(token.shape, F32)
    out[...] = jnp.dot(g9t[...], x, preferred_element_type=F32) * scale


def weight_grad_call(q, after, slots, g9t, xs, total, scale, channels):
    blocks = len(slots)
    rows, cells = g9t.shape
    lanes = xs[0].shape[1]
    first = slots[0]
    aliased = [] if total is None else [total]
    return pl.pallas_call(
        functools.partial(weight_grad_kernel, len(xs), scale),
        out_shape=[jax.ShapeDtypeStruct((rows, channels), F32), TOKEN],
        grid_spec=pltpu.PrefetchScalarGridSpec(
            num_scalar_prefetch=1,
            grid=(blocks,),
            in_specs=[ANY, VMEM]
            + [pl.BlockSpec((xs[0].shape[0] // blocks, lanes), lambda k, q: (k, 0))] * len(xs)
            + [ANY] * len(aliased),
            out_specs=[pl.BlockSpec((rows, lanes), lambda k, q: (0, q[first + k])), VMEM],
        ),
        input_output_aliases={3 + len(xs): 0} if aliased else {},
        compiler_params=pltpu.CompilerParams(
            dimension_semantics=("arbitrary",), vmem_limit_bytes=12 * MIB
        ),
        cost_estimate=LIGHT,
        name="weight_grad",
    )(q, after, g9t, *xs, *aliased)


def last_sum_kernel(core, product, ahead, behind, keep, send):
    part = keep.shape[1]
    total = (product[...] + ahead[...].astype(F32) + behind[...].astype(F32)).astype(BF16)
    for c, (first, second) in enumerate(((keep, send), (send, keep))):

        @pl.when(core[0] == c)
        def _(first=first, second=second):
            first[...] = total[:, :part]
            second[...] = total[:, part:]


def last_sum_call(core, product, ahead, behind):
    cells, lanes = product.shape
    return pl.pallas_call(
        last_sum_kernel,
        out_shape=[jax.ShapeDtypeStruct((cells, lanes // 2), BF16)] * 2,
        in_specs=[SMEM] + [VMEM] * 3,
        out_specs=[VMEM] * 2,
        compiler_params=pltpu.CompilerParams(vmem_limit_bytes=4 * MIB),
        cost_estimate=LIGHT,
        name="last_sum",
    )(core, product, ahead, behind)


def join_kernel(core, after, keep, other, out):
    for c, order in enumerate(((keep, other), (other, keep))):

        @pl.when(core[0] == c)
        def _(order=order):
            out[...] = jnp.transpose(jnp.concatenate([v[...] for v in order], axis=0))


def join_call(core, after, keep, other):
    cells, part = keep.shape
    return pl.pallas_call(
        join_kernel,
        out_shape=jax.ShapeDtypeStruct((part, 2 * cells), BF16),
        in_specs=[SMEM, ANY] + [VMEM] * 2,
        out_specs=VMEM,
        compiler_params=pltpu.CompilerParams(vmem_limit_bytes=4 * MIB),
        cost_estimate=LIGHT,
        name="join",
    )(core, after, keep, other)


def body(inputs, weight, bias_vector, cotangent):
    part, cells = inputs.shape
    devices = lax.axis_size("filt")
    case_rows = lax.axis_size("case")
    channels = part * devices
    chips = devices // 2
    half = cells // 2
    lanes = 2 * part
    far = chips // 2
    scale = 1.0 / (cells // FIELD * case_rows)

    cycle = chip_cycle(chips)
    offsets = [0]
    for d in range(1, far):
        offsets += [-d, d]
    offsets.append(far)
    slot = {d: n for n, d in enumerate(offsets)}
    place = {chip: n for n, chip in enumerate(cycle)}
    table = np.array(
        [[cycle[(place[chip] + d) % chips] for d in offsets] for chip in range(chips)], np.int32
    )
    me = lax.axis_index("filt")
    core = me % 2
    q = lax.dynamic_index_in_dim(jnp.asarray(table), me // 2, 0, keepdims=False)

    forwards, backwards = [], []
    for n, chip in enumerate(cycle):
        for c in range(2):
            forwards.append((2 * chip + c, 2 * cycle[(n + 1) % chips] + c))
            backwards.append((2 * chip + c, 2 * cycle[(n - 1) % chips] + c))
    swap = [(n, n ^ 1) for n in range(devices)]
    onward = lambda v: lax.ppermute(v, "filt", forwards)
    back = lambda v: lax.ppermute(v, "filt", backwards)
    sibling = lambda v: lax.ppermute(v, "filt", swap)
    pair = case_rows == 2
    across = lambda v: lax.ppermute(v, "case", [(0, 1), (1, 0)])
    tie = lambda *v: lax.optimization_barrier(v)

    x_t = jnp.transpose(inputs)
    mine = lax.dynamic_slice_in_dim(x_t, core * half, half, 0)
    theirs = sibling(lax.dynamic_slice_in_dim(x_t, (1 - core) * half, half, 0))
    own_block = jnp.where(
        core == 0,
        jnp.concatenate([mine, theirs], axis=1),
        jnp.concatenate([theirs, mine], axis=1),
    )
    block = {0: own_block, -1: onward(own_block), 1: back(own_block)}
    theirs, weight, cotangent, bias_vector = tie(theirs, weight, cotangent, bias_vector)
    w_own, w_sib = weight, sibling(weight)
    cot_t = jnp.transpose(cotangent)
    cot_own = lax.dynamic_slice_in_dim(cot_t, core * half, half, 0)
    cot_sib = sibling(lax.dynamic_slice_in_dim(cot_t, (1 - core) * half, half, 0))
    bias_row = bias_vector[None, :]
    bias_sib = sibling(bias_row)
    block[-1], block[1], cot_sib, bias_sib = tie(block[-1], block[1], cot_sib, bias_sib)
    bias_row = jnp.concatenate([bias_row, bias_sib], axis=1)

    stacks = []

    def stack(ds, parts):
        x = jnp.concatenate(parts, axis=0)
        stacks.append(([slot[d] for d in ds], x, across(x) if pair else None))

    w_all, token = hold_call(w_own, w_sib)
    for s in range(1, far):
        if s > 1:
            block[-s], block[s] = onward(block[-s + 1]), back(block[s - 1])
            if s == far - 1:
                early = offsets[: 2 * far - 3]
                carry, token = forward_call(
                    q, token, [slot[d] for d in early], [block[d] for d in early], w_all, None
                )
            block[-s], token_a = tie(block[-s], token)
            block[s], token_b = tie(block[s], token)
            token = token_a
        if s < far - 1:
            ds = [0, -1, 1] if s == 1 else [-s, s]
            stack(ds, [block[d] for d in ds])
    s = far - 1
    top, low = onward(block[-s][: half // 2]), back(block[s][half // 2 :])
    carry, token = forward_call(q, token, [slot[-s], slot[s]], [block[-s], block[s]], w_all, carry)
    tops = [top, low, token] + [x for _, _, x in stacks[:1] if pair]
    top, low, token, *done = tie(*tops)
    others = done
    act_own, act_sib, g_own, g_sib, g9 = gate_call(
        q, token, [slot[far]], [[top, low]], w_all, carry, bias_row, cot_own, cot_sib
    )

    grad_at = lambda after, ds, dtype, pieces=1: input_grad_call(
        q, after, [slot[d] for d in ds], dtype, pieces, g9, w_all, lanes
    )
    top_p, low_p, after_top = grad_at(token, [far], BF16, 2)
    ahead, behind = onward(top_p), back(low_p)
    act_recv, g_recv = sibling(act_sib), sibling(g_sib)
    after_top, g_recv = tie(after_top, g_recv)
    p_ahead, p_behind, token = grad_at(after_top, [far - 1, -(far - 1)], F32)
    gs = [jnp.concatenate([g_own, g_recv], axis=0)]
    waits = [act_recv, gs[0]] + [x for _, _, x in stacks[1:] if pair]
    ahead, behind, token, act_recv, gs[0], *done = tie(ahead, behind, token, *waits)
    others += done
    if pair:
        gs.append(across(gs[0]))
    stack(
        [-(far - 1), far - 1, far], [block[-(far - 1)], block[far - 1], top, low]
    )
    hop = half // 2
    ahead = jnp.concatenate([p_ahead[:hop] + ahead.astype(F32), p_ahead[hop:]], axis=0)
    behind = jnp.concatenate([p_behind[:hop], p_behind[hop:] + behind.astype(F32)], axis=0)
    ahead, behind = tie(ahead.astype(BF16), behind.astype(BF16))
    ahead, behind = onward(ahead), back(behind)
    rest_ds = [d for n in range(far - 2, 0, -1) for d in (n, -n)] + [0]
    *rest, token = grad_at(token, rest_ds, F32)
    rest = dict(zip(rest_ds, rest))
    ahead, behind, token, *gs = tie(ahead, behind, token, *gs)

    g9t, bias_grad, activated = displaced_call(core[None], token, act_own, act_recv, gs, scale)
    state = {"total": None, "next": 0, "token": token}

    def weight_grads():
        n = state["next"]
        ids, x, _ = stacks[n]
        xs = [x, sibling(x)]
        if pair:
            xs += [others[n], sibling(others[n])]
        state["total"], state["token"] = weight_grad_call(
            q, state["token"], ids, g9t, xs, state["total"], scale, channels
        )
        state["next"] = n + 1
        return state["token"]

    for s in range(far - 2, 0, -1):
        ahead = (rest[s] + ahead.astype(F32)).astype(BF16)
        behind = (rest[-s] + behind.astype(F32)).astype(BF16)
        ahead, behind = tie(ahead, behind)
        ahead, behind = onward(ahead), back(behind)
        waits = [ahead, behind]
        if state["next"] < len(stacks) - 1:
            waits.append(weight_grads())
        else:
            waits.append(state["token"])
        if s == 1 and pair:
            waits.append(stacks[-1][2])
        ahead, behind, state["token"], *last = tie(*waits)
        others += last
    keep, send = last_sum_call(core[None], rest[0], ahead, behind)
    other = sibling(send)
    while state["next"] < len(stacks):
        weight_grads()
    total = state["total"]
    input_grad = join_call(core[None], state["token"], keep, other)
    bias_grad = bias_grad[0]
    if not pair:
        total, bias_grad = lax.psum((total, bias_grad), "case")
    weight_grad = total.reshape(9, part, channels)
    return activated, input_grad, weight_grad, bias_grad


def solution(mesh):
    in_specs = (P("filt", "case"), P(None, "filt", None), P("filt"), P("filt", "case"))
    out_specs = (P("filt", "case"), P("filt", "case"), P(None, "filt", None), P("filt"))
    return jax.shard_map(body, mesh=mesh, in_specs=in_specs, out_specs=out_specs, check_vma=False)
```

```python
import functools

import jax
import jax.numpy as jnp
import numpy as np
from jax import lax
from jax.experimental import pallas as pl
from jax.experimental.pallas import tpu as pltpu
from jax.sharding import PartitionSpec as P

GRID = 24
FIELD = GRID * GRID
STEPS = (-1, 0, 1)
EDGE = 8
F32 = jnp.float32
BF16 = jnp.bfloat16
MIB = 1024 * 1024
LIGHT = pl.CostEstimate(flops=1000, transcendentals=0, bytes_accessed=1000)
VMEM = pl.BlockSpec(memory_space=pltpu.VMEM)
SMEM = pl.BlockSpec(memory_space=pltpu.SMEM)
ANY = pl.BlockSpec(memory_space=pl.ANY)
TOKEN = jax.ShapeDtypeStruct((8, 128), F32)


def chip_cycle(chips):
    rows = 4
    cols = chips // rows
    walk = [(r, 0) for r in range(rows)]
    for r in reversed(range(rows)):
        across = range(1, cols) if (rows - 1 - r) % 2 == 0 else reversed(range(1, cols))
        walk += [(r, c) for c in across]
    return [r * cols + c for r, c in walk]


def rows_moved(v, a):
    if a == 0:
        return v
    gap = jnp.zeros((GRID, v.shape[1]), v.dtype)
    pieces = []
    for s in range(0, v.shape[0], FIELD):
        pieces += [v[s + GRID : s + FIELD], gap] if a > 0 else [gap, v[s : s + FIELD - GRID]]
    return jnp.concatenate(pieces, axis=0)


def grid_columns(cells, lanes):
    r = lax.broadcasted_iota(jnp.int32, (cells, lanes), 0)
    return lax.rem(r, GRID)


def columns_moved(field, v, b, col):
    if b == 0:
        return v
    cells, lanes = v.shape
    field[EDGE : EDGE + cells, :lanes] = v
    moved = field[EDGE + b : EDGE + b + cells, :lanes]
    ok = col >= 1 if b < 0 else col < GRID - 1
    return jnp.where(ok, moved, 0.0)


def clear_edges(field):
    rows, lanes = field.shape
    field[0:EDGE, :] = jnp.zeros((EDGE, lanes), field.dtype)
    field[rows - EDGE : rows, :] = jnp.zeros((EDGE, lanes), field.dtype)


def hold_kernel(w_own, w_sib, out, token, sems):
    part = w_own.shape[1]
    token[...] = jnp.zeros(token.shape, F32)
    copies = [
        pltpu.make_async_copy(w, out.at[:, n * part : (n + 1) * part], sems.at[n])
        for n, w in enumerate((w_own, w_sib))
    ]
    for copy in copies:
        copy.start()
    for copy in copies:
        copy.wait()


def hold_call(w_own, w_sib):
    taps, part, channels = w_own.shape
    return pl.pallas_call(
        hold_kernel,
        out_shape=[jax.ShapeDtypeStruct((taps, 2 * part, channels), BF16), TOKEN],
        in_specs=[pl.BlockSpec(memory_space=pltpu.HBM)] * 2,
        out_specs=[VMEM] * 2,
        scratch_shapes=[pltpu.SemaphoreType.DMA((2,))],
        compiler_params=pltpu.CompilerParams(vmem_limit_bytes=12 * MIB),
        cost_estimate=LIGHT,
        name="hold",
    )(w_own, w_sib)


def forward_sums(q_ref, slots, xs, w_all, carry, b):
    lanes = xs[0][0].shape[1] if isinstance(xs[0], (list, tuple)) else xs[0].shape[1]
    total = None if carry is None else carry
    for a in STEPS:
        tap = (a + 1) * 3 + b + 1
        part = None
        for n, x in zip(slots, xs):
            cols = pl.ds(pl.multiple_of(q_ref[n] * lanes, lanes), lanes)
            w = w_all[tap, :, cols]
            v = jnp.concatenate([p[...] for p in x], axis=0) if isinstance(x, (list, tuple)) else x[...]
            y = lax.dot_general(v, w, (((1,), (1,)), ((), ())), preferred_element_type=F32)
            part = y if part is None else part + y
        part = rows_moved(part, a)
        total = part if total is None else total + part
    return total


def forward_kernel(slots, has_carry, q_ref, after, w_all, *refs):
    refs = list(refs)
    carry = refs.pop(0) if has_carry else None
    xs, out, token = refs[:-2], refs[-2], refs[-1]
    token[...] = jnp.zeros(token.shape, F32)
    for b in STEPS:
        before = carry[b + 1] if has_carry else None
        out[b + 1] = forward_sums(q_ref, slots, xs, w_all, before, b)


def forward_call(q, after, slots, xs, w_all, carry):
    cells, lanes = xs[0].shape
    outs = w_all.shape[1]
    args = ([] if carry is None else [carry]) + list(xs)
    return pl.pallas_call(
        functools.partial(forward_kernel, slots, carry is not None),
        out_shape=[jax.ShapeDtypeStruct((3, cells, outs), F32), TOKEN],
        in_specs=[SMEM, ANY] + [VMEM] * (1 + len(args)),
        out_specs=[VMEM] * 2,
        compiler_params=pltpu.CompilerParams(vmem_limit_bytes=8 * MIB),
        cost_estimate=LIGHT,
        name="forward",
    )(q, after, w_all, *args)


def gate_kernel(slots, halves, q_ref, after, w_all, carry, bias, cot_own, cot_sib, *refs):
    xs = refs[: len(slots) * halves]
    act_own, act_sib, g_own, g_sib, g9, field = refs[len(slots) * halves :]
    xs = [xs[n : n + halves] for n in range(0, len(xs), halves)]
    cells = act_own.shape[0]
    part = act_own.shape[1]
    lanes = 2 * part
    col = grid_columns(cells, lanes)
    clear_edges(field)
    preact = bias[0:1, :]
    for b in (0, -1, 1):
        sums = forward_sums(q_ref, slots, xs, w_all, carry[b + 1], b)
        preact = preact + columns_moved(field, sums, b, col)
    gate = jax.nn.sigmoid(preact)
    act = (preact * gate).astype(BF16)
    act_own[...], act_sib[...] = act[:, :part], act[:, part:]
    cot = jnp.concatenate([cot_own[...], cot_sib[...]], axis=1).astype(F32)
    grad = (cot * gate * (1.0 + preact * (1.0 - gate))).astype(BF16)
    g_own[...], g_sib[...] = grad[:, :part], grad[:, part:]
    grad = grad.astype(F32)
    for b in STEPS:
        side = columns_moved(field, grad, -b, col)
        for a in STEPS:
            tap = (a + 1) * 3 + b + 1
            g9[:, tap * lanes : (tap + 1) * lanes] = rows_moved(side, -a).astype(BF16)


def gate_call(q, after, slots, xs, w_all, carry, bias, cot_own, cot_sib):
    cells = carry.shape[1]
    outs = carry.shape[2]
    part = outs // 2
    halves = len(xs[0])
    flat = [p for x in xs for p in x]
    piece = jax.ShapeDtypeStruct((cells, part), BF16)
    return pl.pallas_call(
        functools.partial(gate_kernel, slots, halves),
        out_shape=[piece] * 4 + [jax.ShapeDtypeStruct((cells, 9 * outs), BF16)],
        in_specs=[SMEM, ANY] + [VMEM] * (5 + len(flat)),
        out_specs=[VMEM] * 5,
        scratch_shapes=[pltpu.VMEM((cells + 2 * EDGE, outs), F32)],
        compiler_params=pltpu.CompilerParams(vmem_limit_bytes=10 * MIB),
        cost_estimate=LIGHT,
        name="gate",
    )(q, after, w_all, carry, bias, cot_own, cot_sib, *flat)


def input_grad_kernel(slots, pieces, q_ref, after, w_all, g9, *outs):
    lanes = outs[0].shape[1]
    outs = list(outs)
    token = outs.pop()
    token[...] = jnp.zeros(token.shape, F32)
    for n in slots:
        cols = pl.ds(pl.multiple_of(q_ref[n] * lanes, lanes), lanes)
        w = w_all[:, :, cols].reshape(-1, lanes)
        total = jnp.dot(g9[...], w, preferred_element_type=F32)
        rows = total.shape[0] // pieces
        for p in range(pieces):
            out = outs.pop(0)
            out[...] = total[p * rows : (p + 1) * rows].astype(out.dtype)


def input_grad_call(q, after, slots, dtype, pieces, g9, w_all, lanes):
    cells, depth = g9.shape
    count = len(slots) * pieces
    return pl.pallas_call(
        functools.partial(input_grad_kernel, slots, pieces),
        out_shape=[jax.ShapeDtypeStruct((cells // pieces, lanes), dtype)] * count + [TOKEN],
        in_specs=[SMEM, ANY] + [VMEM] * 2,
        out_specs=[VMEM] * (count + 1),
        compiler_params=pltpu.CompilerParams(vmem_limit_bytes=8 * MIB),
        cost_estimate=LIGHT,
        name="input_grad",
    )(q, after, w_all, g9)


def displaced_kernel(scale, core, after, act_own, act_sib, *refs):
    gs = refs[:-4]
    out, bias_out, act_out, field = refs[-4:]
    for c, order in enumerate(((act_own, act_sib), (act_sib, act_own))):

        @pl.when(core[0] == c)
        def _(order=order):
            act_out[...] = jnp.transpose(jnp.concatenate([v[...] for v in order], axis=0))

    cells = out.shape[1]
    part = out.shape[0] // 9
    clear_edges(field)
    grad = jnp.concatenate([g[...] for g in gs], axis=0).astype(F32)
    bias_out[...] = jnp.sum(grad, axis=0, keepdims=True) * scale
    col = grid_columns(cells, part)
    for b in STEPS:
        side = columns_moved(field, grad, -b, col)
        for a in STEPS:
            tap = (a + 1) * 3 + b + 1
            moved = rows_moved(side, -a).astype(BF16)
            out[tap * part : (tap + 1) * part, :] = jnp.transpose(moved)


def displaced_call(core, after, act_own, act_sib, gs, scale):
    cells = sum(g.shape[0] for g in gs)
    part = gs[0].shape[1]
    return pl.pallas_call(
        functools.partial(displaced_kernel, scale),
        out_shape=[
            jax.ShapeDtypeStruct((9 * part, cells), BF16),
            jax.ShapeDtypeStruct((1, part), F32),
            jax.ShapeDtypeStruct((part, 2 * act_own.shape[0]), BF16),
        ],
        in_specs=[SMEM, ANY] + [VMEM] * (2 + len(gs)),
        out_specs=[VMEM] * 3,
        scratch_shapes=[pltpu.VMEM((cells + 2 * EDGE, part), F32)],
        compiler_params=pltpu.CompilerParams(vmem_limit_bytes=10 * MIB),
        cost_estimate=LIGHT,
        name="displaced",
    )(core, after, act_own, act_sib, *gs)


def weight_grad_kernel(places, scale, q_ref, after, g9t, *refs):
    x = jnp.concatenate([x[...] for x in refs[:places]], axis=0)
    out, token = refs[-2:]
    token[...] = jnp.zeros(token.shape, F32)
    out[...] = jnp.dot(g9t[...], x, preferred_element_type=F32) * scale


def weight_grad_call(q, after, slots, g9t, xs, total, scale, channels):
    blocks = len(slots)
    rows, cells = g9t.shape
    lanes = xs[0].shape[1]
    first = slots[0]
    aliased = [] if total is None else [total]
    return pl.pallas_call(
        functools.partial(weight_grad_kernel, len(xs), scale),
        out_shape=[jax.ShapeDtypeStruct((rows, channels), F32), TOKEN],
        grid_spec=pltpu.PrefetchScalarGridSpec(
            num_scalar_prefetch=1,
            grid=(blocks,),
            in_specs=[ANY, VMEM]
            + [pl.BlockSpec((xs[0].shape[0] // blocks, lanes), lambda k, q: (k, 0))] * len(xs)
            + [ANY] * len(aliased),
            out_specs=[pl.BlockSpec((rows, lanes), lambda k, q: (0, q[first + k])), VMEM],
        ),
        input_output_aliases={3 + len(xs): 0} if aliased else {},
        compiler_params=pltpu.CompilerParams(
            dimension_semantics=("arbitrary",), vmem_limit_bytes=12 * MIB
        ),
        cost_estimate=LIGHT,
        name="weight_grad",
    )(q, after, g9t, *xs, *aliased)


def last_sum_kernel(core, product, ahead, behind, keep, send):
    part = keep.shape[1]
    total = (product[...] + ahead[...].astype(F32) + behind[...].astype(F32)).astype(BF16)
    for c, (first, second) in enumerate(((keep, send), (send, keep))):

        @pl.when(core[0] == c)
        def _(first=first, second=second):
            first[...] = total[:, :part]
            second[...] = total[:, part:]


def last_sum_call(core, product, ahead, behind):
    cells, lanes = product.shape
    return pl.pallas_call(
        last_sum_kernel,
        out_shape=[jax.ShapeDtypeStruct((cells, lanes // 2), BF16)] * 2,
        in_specs=[SMEM] + [VMEM] * 3,
        out_specs=[VMEM] * 2,
        compiler_params=pltpu.CompilerParams(vmem_limit_bytes=4 * MIB),
        cost_estimate=LIGHT,
        name="last_sum",
    )(core, product, ahead, behind)


def join_kernel(core, after, keep, other, out):
    for c, order in enumerate(((keep, other), (other, keep))):

        @pl.when(core[0] == c)
        def _(order=order):
            out[...] = jnp.transpose(jnp.concatenate([v[...] for v in order], axis=0))


def join_call(core, after, keep, other):
    cells, part = keep.shape
    return pl.pallas_call(
        join_kernel,
        out_shape=jax.ShapeDtypeStruct((part, 2 * cells), BF16),
        in_specs=[SMEM, ANY] + [VMEM] * 2,
        out_specs=VMEM,
        compiler_params=pltpu.CompilerParams(vmem_limit_bytes=4 * MIB),
        cost_estimate=LIGHT,
        name="join",
    )(core, after, keep, other)


def body(inputs, weight, bias_vector, cotangent):
    part, cells = inputs.shape
    devices = lax.axis_size("filt")
    case_rows = lax.axis_size("case")
    channels = part * devices
    chips = devices // 2
    half = cells // 2
    lanes = 2 * part
    far = chips // 2
    scale = 1.0 / (cells // FIELD * case_rows)

    cycle = chip_cycle(chips)
    offsets = [0]
    for d in range(1, far):
        offsets += [-d, d]
    offsets.append(far)
    slot = {d: n for n, d in enumerate(offsets)}
    place = {chip: n for n, chip in enumerate(cycle)}
    table = np.array(
        [[cycle[(place[chip] + d) % chips] for d in offsets] for chip in range(chips)], np.int32
    )
    me = lax.axis_index("filt")
    core = me % 2
    q = lax.dynamic_index_in_dim(jnp.asarray(table), me // 2, 0, keepdims=False)

    forwards, backwards = [], []
    for n, chip in enumerate(cycle):
        for c in range(2):
            forwards.append((2 * chip + c, 2 * cycle[(n + 1) % chips] + c))
            backwards.append((2 * chip + c, 2 * cycle[(n - 1) % chips] + c))
    swap = [(n, n ^ 1) for n in range(devices)]
    onward = lambda v: lax.ppermute(v, "filt", forwards)
    back = lambda v: lax.ppermute(v, "filt", backwards)
    sibling = lambda v: lax.ppermute(v, "filt", swap)
    pair = case_rows == 2
    across = lambda v: lax.ppermute(v, "case", [(0, 1), (1, 0)])
    tie = lambda *v: lax.optimization_barrier(v)

    x_t = jnp.transpose(inputs)
    mine = lax.dynamic_slice_in_dim(x_t, core * half, half, 0)
    theirs = sibling(lax.dynamic_slice_in_dim(x_t, (1 - core) * half, half, 0))
    own_block = jnp.where(
        core == 0,
        jnp.concatenate([mine, theirs], axis=1),
        jnp.concatenate([theirs, mine], axis=1),
    )
    block = {0: own_block, -1: onward(own_block), 1: back(own_block)}
    theirs, weight, cotangent, bias_vector = tie(theirs, weight, cotangent, bias_vector)
    w_own, w_sib = weight, sibling(weight)
    cot_t = jnp.transpose(cotangent)
    cot_own = lax.dynamic_slice_in_dim(cot_t, core * half, half, 0)
    cot_sib = sibling(lax.dynamic_slice_in_dim(cot_t, (1 - core) * half, half, 0))
    bias_row = bias_vector[None, :]
    bias_sib = sibling(bias_row)
    block[-1], block[1], cot_sib, bias_sib = tie(block[-1], block[1], cot_sib, bias_sib)
    bias_row = jnp.concatenate([bias_row, bias_sib], axis=1)

    stacks = []

    def stack(ds, parts):
        x = jnp.concatenate(parts, axis=0)
        stacks.append(([slot[d] for d in ds], x, across(x) if pair else None))

    w_all, token = hold_call(w_own, w_sib)
    for s in range(1, far):
        if s > 1:
            block[-s], block[s] = onward(block[-s + 1]), back(block[s - 1])
            if s == far - 1:
                early = offsets[: 2 * far - 3]
                carry, token = forward_call(
                    q, token, [slot[d] for d in early], [block[d] for d in early], w_all, None
                )
            block[-s], token_a = tie(block[-s], token)
            block[s], token_b = tie(block[s], token)
            token = token_a
        if s < far - 1:
            ds = [0, -1, 1] if s == 1 else [-s, s]
            stack(ds, [block[d] for d in ds])
    s = far - 1
    top, low = onward(block[-s][: half // 2]), back(block[s][half // 2 :])
    carry, token = forward_call(q, token, [slot[-s], slot[s]], [block[-s], block[s]], w_all, carry)
    tops = [top, low, token] + [x for _, _, x in stacks[:1] if pair]
    top, low, token, *done = tie(*tops)
    others = done
    act_own, act_sib, g_own, g_sib, g9 = gate_call(
        q, token, [slot[far]], [[top, low]], w_all, carry, bias_row, cot_own, cot_sib
    )

    grad_at = lambda after, ds, dtype, pieces=1: input_grad_call(
        q, after, [slot[d] for d in ds], dtype, pieces, g9, w_all, lanes
    )
    top_p, low_p, after_top = grad_at(token, [far], BF16, 2)
    ahead, behind = onward(top_p), back(low_p)
    act_recv, g_recv = sibling(act_sib), sibling(g_sib)
    after_top, g_recv = tie(after_top, g_recv)
    p_ahead, p_behind, token = grad_at(after_top, [far - 1, -(far - 1)], F32)
    gs = [jnp.concatenate([g_own, g_recv], axis=0)]
    waits = [act_recv, gs[0]] + [x for _, _, x in stacks[1:] if pair]
    ahead, token, act_recv, gs[0], *done = tie(ahead, token, *waits)
    behind, token = tie(behind, token)
    others += done
    if pair:
        gs.append(across(gs[0]))
    stack(
        [-(far - 1), far - 1, far], [block[-(far - 1)], block[far - 1], top, low]
    )
    hop = half // 2
    ahead = jnp.concatenate([p_ahead[:hop] + ahead.astype(F32), p_ahead[hop:]], axis=0)
    behind = jnp.concatenate([p_behind[:hop], p_behind[hop:] + behind.astype(F32)], axis=0)
    ahead, behind = onward(ahead.astype(BF16)), back(behind.astype(BF16))
    rest_ds = [d for n in range(far - 2, 0, -1) for d in (n, -n)] + [0]
    *rest, token = grad_at(token, rest_ds, F32)
    rest = dict(zip(rest_ds, rest))
    ahead, token, *gs = tie(ahead, token, *gs)
    behind, token = tie(behind, token)

    g9t, bias_grad, activated = displaced_call(core[None], token, act_own, act_recv, gs, scale)
    state = {"total": None, "next": 0, "token": token}

    def weight_grads():
        n = state["next"]
        ids, x, _ = stacks[n]
        xs = [x, sibling(x)]
        if pair:
            xs += [others[n], sibling(others[n])]
        state["total"], state["token"] = weight_grad_call(
            q, state["token"], ids, g9t, xs, state["total"], scale, channels
        )
        state["next"] = n + 1
        return state["token"]

    for s in range(far - 2, 0, -1):
        ahead = (rest[s] + ahead.astype(F32)).astype(BF16)
        behind = (rest[-s] + behind.astype(F32)).astype(BF16)
        ahead, behind = tie(ahead, behind)
        ahead, behind = onward(ahead), back(behind)
        waits = [ahead, behind]
        if state["next"] < len(stacks) - 1:
            waits.append(weight_grads())
        else:
            waits.append(state["token"])
        if s == 1 and pair:
            waits.append(stacks[-1][2])
        ahead, behind, state["token"], *last = tie(*waits)
        others += last
    keep, send = last_sum_call(core[None], rest[0], ahead, behind)
    other = sibling(send)
    while state["next"] < len(stacks):
        weight_grads()
    total = state["total"]
    input_grad = join_call(core[None], state["token"], keep, other)
    bias_grad = bias_grad[0]
    if not pair:
        total, bias_grad = lax.psum((total, bias_grad), "case")
    weight_grad = total.reshape(9, part, channels)
    return activated, input_grad, weight_grad, bias_grad


def solution(mesh):
    in_specs = (P("filt", "case"), P(None, "filt", None), P("filt"), P("filt", "case"))
    out_specs = (P("filt", "case"), P("filt", "case"), P(None, "filt", None), P("filt"))
    return jax.shard_map(body, mesh=mesh, in_specs=in_specs, out_specs=out_specs, check_vma=False)
```
